512 devices in a mesh: tile: 16 (over y, x), cuts: 32 (over z, core).
Axes of the slice: x: 4, y: 4, z: 16, core: 2. Of those that a mesh axis runs over, the one named last changes fastest.
Arguments:
- density: bfloat16 [128, 2048, 1024], P('cuts', 'tile'), may hold values from -8 to 8
- valid: int32 [2048, 1024], P('tile'), may hold values from 0 to 1, as said below
- row_taps: bfloat16 [4, 128, 17], P(None, 'cuts'), may hold values from -1.5 to 1.5
- col_taps: bfloat16 [4, 128, 17], P(None, 'cuts'), may hold values from -1.5 to 1.5
- amp_matrix: bfloat16 [128, 128], replicated, may hold values from -0.5 to 0.5
- like_matrix: bfloat16 [128, 128], replicated, may hold values from -0.5 to 0.5
Outputs:
- amplitude: bfloat16 [128, 2097152], P(None, ('tile', 'cuts'))
- likelihood: bfloat16 [128, 2097152], P(None, ('tile', 'cuts'))
The draws below stay inside these ranges and needn't reach their ends.
Inputs may be any that keep to these rules, and one draw needn't show every extreme that they name: Every pixel row holds at least one valid pixel; the share of valid pixels rises from about 0.3 in the first row to about 0.9 in the last.
All inputs are finite; a program needn't handle non-finite values.
Results may differ from the reference program's by a relative error of at most 0.0082.
Values may be sent and summed in bfloat16 or wider, within the bound.
A program may use at most 64 MiB of HBM per device.

```python
import jax
import jax.numpy as jnp
from jax import lax

SLICES = 128
ZBINS = 128
TERMS = 4
REACH = 8
COLS = 1024
NROWS = 2048


def draw_valid(key, part):
    row_index = lax.broadcasted_iota(jnp.int32, (NROWS, COLS), 0)
    col_index = lax.broadcasted_iota(jnp.int32, (NROWS, COLS), 1)
    limit = 300 + 600 * row_index // max(NROWS - 1, 1)
    picks = jax.random.randint(key, (NROWS, COLS), 0, 1000)
    keeps = (picks < limit) | (col_index == row_index % COLS)
    return keeps.astype(jnp.int32)


def draw_density(key, part):
    own_key = jax.random.fold_in(key, 11)
    key_offset, key_offsign, key_noise = jax.random.split(own_key, 3)
    magnitude = jax.random.uniform(key_offset, (SLICES, 1, 1), jnp.float32, 0.5, 2.0)
    offset_sign = jnp.where(jax.random.bernoulli(key_offsign, 0.5, (SLICES, 1, 1)), 1.0, -1.0)
    offsets = offset_sign * magnitude
    values = offsets + jax.random.normal(key_noise, (SLICES, NROWS, COLS), jnp.float32)
    return jnp.clip(values, -8.0, 8.0).astype(jnp.bfloat16)


def shard_levels(stream_key, dims, cuts, least, largest):
    def one(axis_at, parts):
        draws = jax.random.uniform(jax.random.fold_in(jax.random.fold_in(stream_key, 6), axis_at), (parts,), jnp.float32, least / len(cuts), largest / len(cuts))
        return jnp.repeat(jnp.exp(draws), dims[axis_at] // parts).reshape((-1,) + (1,) * (len(dims) - axis_at - 1))

    gain = one(*cuts[0])
    for cut in cuts[1:]:
        gain = gain * one(*cut)
    return gain


def scatter_about(key, extent, width, bound, shards=(), dtype=jnp.bfloat16):
    loudness = shard_levels(key, extent, shards, -0.22, 0.18) if shards else 1.0
    array = jax.random.normal(key, extent, jnp.float32) * width * loudness
    return jnp.minimum(jnp.maximum(array, -bound), bound).astype(dtype)


def setup_inputs(seed: int = 0) -> dict:
    streams_of = jax.random.split(jax.random.key(seed), 7)
    density = draw_density(jax.random.fold_in(streams_of[6], 71), 0)
    valid = draw_valid(jax.random.fold_in(streams_of[6], 71), 0)
    row_taps = scatter_about(streams_of[2], (TERMS, SLICES, 2 * REACH + 1), (2 * REACH + 1) ** -0.5, 1.5, ((1, 32),))
    col_taps = scatter_about(streams_of[3], (TERMS, SLICES, 2 * REACH + 1), (2 * REACH + 1) ** -0.5, 1.5, ((1, 32),))
    amp_matrix = scatter_about(streams_of[4], (SLICES, ZBINS), SLICES ** -0.5, 0.5)
    like_matrix = scatter_about(streams_of[5], (SLICES, ZBINS), SLICES ** -0.5, 0.5)
    return {"density": density, "valid": valid, "row_taps": row_taps, "col_taps": col_taps, "amp_matrix": amp_matrix, "like_matrix": like_matrix}


def smooth_axis(plane, taps, axis):
    length = plane.shape[axis]
    widths = [(0, 0), (0, 0)]
    widths[axis] = (REACH, REACH)
    padded = jnp.pad(plane, widths)
    total = jnp.zeros(plane.shape, jnp.float32)
    for offset in range(2 * REACH + 1):
        shifted = lax.slice_in_dim(padded, offset, offset + length, axis=axis)
        total = total + taps[offset].astype(jnp.float32) * shifted
    return total


def filter_slice(packed):
    plane, row_set, col_set = packed
    plane_float = plane.astype(jnp.float32)
    total = jnp.zeros(plane.shape, jnp.float32)
    for term in range(TERMS):
        rowed = smooth_axis(plane_float, row_set[term], 0).astype(jnp.bfloat16)
        total = total + smooth_axis(rowed.astype(jnp.float32), col_set[term], 1)
    return total.astype(jnp.bfloat16)


def project_block(block, amp_matrix, like_matrix):
    amp_float = jnp.dot(amp_matrix.T, block, preferred_element_type=jnp.float32)
    like_float = amp_float * jnp.dot(like_matrix.T, block, preferred_element_type=jnp.float32)
    return amp_float.astype(jnp.bfloat16), like_float.astype(jnp.bfloat16)


def reference(density, valid, row_taps, col_taps, amp_matrix, like_matrix):
    mask_float = valid.astype(jnp.float32)
    sums = jnp.sum(density.astype(jnp.float32) * mask_float[None], axis=(1, 2))
    background = sums / jnp.sum(mask_float)
    masked_field = (mask_float[None] * (density.astype(jnp.float32) - background[:, None, None])).astype(jnp.bfloat16)
    filtered = lax.map(filter_slice, (masked_field, jnp.moveaxis(row_taps, 1, 0), jnp.moveaxis(col_taps, 1, 0)))
    flat = filtered.reshape(SLICES, NROWS * COLS)
    blocks = flat.reshape(SLICES, NROWS, COLS).transpose(1, 0, 2)
    amp_blocks, like_blocks = lax.map(lambda block: project_block(block, amp_matrix, like_matrix), blocks)
    amplitude = amp_blocks.transpose(1, 0, 2).reshape(ZBINS, NROWS * COLS)
    likelihood = like_blocks.transpose(1, 0, 2).reshape(ZBINS, NROWS * COLS)
    return amplitude, likelihood
```

```python
import functools

import jax
import jax.numpy as jnp
from jax import lax
from jax.experimental import pallas as pl
from jax.experimental.pallas import tpu as pltpu
from jax.sharding import PartitionSpec as P

MESH = pl.DeviceIdType.MESH
REACH = 8
TAPS = 2 * REACH + 1
ABSENT = 1024.0
F32 = jnp.float32
BF16 = jnp.bfloat16


def distance(p):
    return (8 - (p + 1) // 2) * (2 * (p % 2) - 1)


def exchange_kernel(
    dens, valid, rtap, ctap, amp, like,
    recv, wout,
    base, rband, cband, field, wide, outs, send, stat, stats, bgs, hsend, hrecv, wmat,
    stat_ssem, stat_rsem, halo_ssem, halo_rsem, ssem, rsem, wsem, osem,
):
    n_s, n_row, n_col = dens.shape
    n_tile, n_cut = lax.axis_size("tile"), lax.axis_size("cuts")
    n_z = n_cut // 2
    tile, me = lax.axis_index("tile"), lax.axis_index("cuts")
    z, core = me // 2, me % 2
    n_a = n_col // 128

    barrier = pltpu.get_barrier_semaphore()
    for i in range(1, n_tile):
        pl.semaphore_signal(barrier, inc=1, device_id={"tile": (tile + i) % n_tile}, device_id_type=MESH)
    for i in range(1, n_cut):
        pl.semaphore_signal(barrier, inc=1, device_id={"cuts": (me + i) % n_cut}, device_id_type=MESH)

    def fold(x):
        x = x[0:8] + x[8:16]
        total = x[:, 0:128]
        for a in range(1, n_a):
            total = total + x[:, 128 * a : 128 * a + 128]
        return total

    def sum_rows(i, accs):
        rows = pl.ds(pl.multiple_of(i * 16, 16), 16)
        mask = valid[rows, :].astype(F32)
        out = [accs[s] + fold(dens[s, rows, :].astype(F32) * mask) for s in range(n_s)]
        return (*out, accs[n_s] + fold(mask))

    accs = lax.fori_loop(0, n_row // 16, sum_rows, tuple(jnp.zeros((8, 128), F32) for _ in range(n_s + 1)))
    stat[...] = jnp.zeros_like(stat)
    for s in range(n_s + 1):
        stat[s : s + 1, :] = jnp.sum(accs[s], axis=0, keepdims=True)

    top, low = valid[0:8, :] != 0, valid[n_row - 8 : n_row, :] != 0
    for s in range(n_s):
        hsend[0, s] = jnp.where(top, dens[s, 0:16, :].astype(F32)[0:8], ABSENT).astype(BF16)
        hsend[1, s] = jnp.where(low, dens[s, n_row - 16 : n_row, :].astype(F32)[8:16], ABSENT).astype(BF16)

    pl.semaphore_wait(barrier, n_tile - 1 + n_cut - 1)

    stat_copies = []
    for i in range(1, n_tile):
        stat_copies.append(
            pltpu.make_async_remote_copy(
                stat, stats.at[i], stat_ssem.at[i], stat_rsem.at[i],
                device_id={"tile": (tile + i) % n_tile}, device_id_type=MESH,
            )
        )
    halo_copies = []
    for side, step in ((0, n_tile - 1), (1, 1)):
        halo_copies.append(
            pltpu.make_async_remote_copy(
                hsend.at[side], hrecv.at[side], halo_ssem.at[side], halo_rsem.at[side],
                device_id={"tile": (tile + step) % n_tile}, device_id_type=MESH,
            )
        )
    for copy in stat_copies + halo_copies:
        copy.start()

    base[...] = jnp.zeros_like(base)
    for k in range(4):
        base[4 * k : 4 * k + 4, 0:TAPS] = rtap[k].astype(F32)
        base[16 + 4 * k : 20 + 4 * k, 0:TAPS] = ctap[k].astype(F32)
    base[...] = pltpu.roll(base[...], 256 - REACH, 1)

    def build(k, carry):
        for s in range(n_s):
            row = jnp.broadcast_to(base[pl.ds(4 * k + s, 1), :], (8, 256))
            row = pltpu.roll(row, 0, 1, stride=1, stride_axis=0)
            if s % 2:
                row = pltpu.roll(row, 4, 0)
            for p in range(0, n_z, 2):
                pair = [pltpu.roll(row, 8 * ((z + distance(p + i) + n_z) % n_z), 1) for i in range(2)]
                rows = pl.ds(pl.multiple_of(32 * k + 8 * (p % 4), 16), 16)
                rband[s, p // 4, rows, :] = jnp.concatenate(pair, axis=0).astype(BF16)
            col = jnp.broadcast_to(base[pl.ds(16 + 4 * k + s, 1), :], (8, 256))
            col = pltpu.roll(col, 0, 1, stride=1, stride_axis=0)
            lanes = pl.ds(pl.multiple_of(256 * k, 256), 256)
            for m in range(0, 16, 2):
                pair = [pltpu.roll(col, 8 * (m + i), 1) if m + i else col for i in range(2)]
                cband[s, 8 * m : 8 * m + 16, lanes] = jnp.concatenate(pair, axis=0).astype(BF16)
        return carry

    lax.fori_loop(0, 4, build, 0)
    for s in range(n_s):
        field[s, n_row : 2 * n_row, :] = jnp.zeros((n_row, n_col), BF16)

    for copy in stat_copies:
        copy.wait()
    total = stat[...]
    for i in range(1, n_tile):
        total = total + stats[i]
    total = jnp.broadcast_to(jnp.sum(total, axis=1, keepdims=True), (8, 128))
    bgs[...] = total / jnp.broadcast_to(total[n_s : n_s + 1, :], (8, 128))

    def level(s):
        return jnp.concatenate([bgs[pl.ds(s, 1), :]] * n_a, axis=1)

    def mask_rows(i, carry):
        rows = pl.ds(pl.multiple_of(i * 16, 16), 16)
        mask = valid[rows, :].astype(F32)
        for s in range(n_s):
            field[s, rows, :] = (mask * (dens[s, rows, :].astype(F32) - level(s))).astype(BF16)
        return carry

    lax.fori_loop(0, n_row // 16, mask_rows, 0)
    for copy in halo_copies:
        copy.wait()
    has_after = (tile < n_tile - 1).astype(F32)
    has_before = (tile > 0).astype(F32)
    for s in range(n_s):
        after, before = hrecv[0, s].astype(F32), hrecv[1, s].astype(F32)
        after = jnp.where(after > 0.5 * ABSENT, 0.0, after - level(s)) * has_after
        before = jnp.where(before > 0.5 * ABSENT, 0.0, before - level(s)) * has_before
        none = jnp.zeros((8, n_col), F32)
        field[s, n_row : n_row + 16, :] = jnp.concatenate([after, none], axis=0).astype(BF16)
        field[s, 2 * n_row - 16 : 2 * n_row, :] = jnp.concatenate([none, before], axis=0).astype(BF16)

    def block_copy(p, c):
        target = 2 * ((z + distance(p) + n_z) % n_z) + c
        return pltpu.make_async_remote_copy(
            send.at[p, c], recv.at[p, core], ssem.at[p, c], rsem.at[p, core],
            device_id={"cuts": target}, device_id_type=MESH,
        )

    lane = lax.broadcasted_iota(jnp.int32, (32, 128), 1)
    first = lax.broadcasted_iota(jnp.int32, (8, 128), 0) < 4

    def chunk(q, carry):
        for s in range(n_s):
            rowed = jnp.dot(rband[s, q], field[s], preferred_element_type=F32)
            for k in range(4):
                tiles = [rowed[32 * k : 32 * k + 32, 128 * a : 128 * a + 128] for a in range(n_a)]
                for a in range(n_a):
                    right = tiles[a + 1] if a + 1 < n_a else jnp.zeros((32, 128), F32)
                    left = tiles[a - 1] if a else jnp.zeros((32, 128), F32)
                    wide[s, a, :, 256 * k : 256 * k + 128] = tiles[a].astype(BF16)
                    wide[s, a, :, 256 * k + 128 : 256 * k + 256] = jnp.where(lane < 64, right, left).astype(BF16)
            done = lax.dot_general(
                wide[s].reshape(32 * n_a, 1024), cband[s], (((1,), (1,)), ((), ())), preferred_element_type=F32
            )
            outs[s] = done.reshape(n_a, 32, 128)
        for i in range(4):
            p = 4 * q + i
            for a in range(n_a):
                part = [outs[s, a, 8 * i : 8 * i + 8, :] for s in range(n_s)]
                even = [jnp.where(first, part[0], part[1]), jnp.where(first, part[2], part[3])]
                odd = [jnp.where(first, part[1], part[0]), jnp.where(first, part[3], part[2])]
                send[p, 0, :, 128 * a : 128 * a + 128] = jnp.concatenate(even, axis=0).astype(BF16)
                send[p, 1, :, 128 * a : 128 * a + 128] = jnp.concatenate(odd, axis=0).astype(BF16)
        for i in range(4):
            p = 4 * q + i
            for c in range(2):

                @pl.when(jnp.logical_or(p < n_z - 1, c != core))
                def _():
                    block_copy(p, c).start()

        return carry

    lax.fori_loop(0, n_z // 4, chunk, 0)
    own = pltpu.make_async_copy(send.at[n_z - 1, core], recv.at[n_z - 1, core], osem)
    own.start()

    both = jnp.concatenate([amp[...].astype(F32).T, like[...].astype(F32).T], axis=0).astype(BF16)
    at = lax.broadcasted_iota(jnp.int32, (8, 512), 1)
    pos = at >> 5
    dist = (8 - ((pos + 1) >> 1)) * (2 * (pos & 1) - 1)
    inner = (at >> 2) & 3
    inner = inner + core * (1 - 2 * (inner & 1))
    slices = 8 * ((z - dist + 2 * n_z) & (n_z - 1)) + 4 * ((at >> 4) & 1) + inner
    slices = jnp.concatenate([slices] * 16, axis=0)
    row_of = jnp.concatenate([at & 3] * 16, axis=0)
    wanted = slices == lax.broadcasted_iota(jnp.int32, (128, 512), 0)
    for r in range(4):
        pick = jnp.where(jnp.logical_and(wanted, row_of == r), 1.0, 0.0).astype(BF16)
        wmat[256 * r : 256 * r + 256, :] = jnp.dot(both, pick, preferred_element_type=F32).astype(BF16)
    put = pltpu.make_async_copy(wmat, wout, wsem)
    put.start()

    own.wait()
    put.wait()

    def finish(p, carry):
        for c in range(2):

            @pl.when(jnp.logical_or(p < n_z - 1, c != core))
            def _():
                block_copy(p, c).wait_send()
                pltpu.make_async_remote_copy(
                    send.at[p, c], recv.at[p, c], ssem.at[p, c], rsem.at[p, c],
                    device_id={"cuts": me}, device_id_type=MESH,
                ).wait_recv()

        return carry

    lax.fori_loop(0, n_z, finish, 0)


def project_kernel(blocks, weights, amp_out, like_out):
    for j in range(4):
        both = jnp.dot(weights[...], blocks[:, 256 * j : 256 * j + 256], preferred_element_type=F32)
        for r in range(4):
            amp_float = both[256 * r : 256 * r + 128]
            like_float = amp_float * both[256 * r + 128 : 256 * r + 256]
            at = 1024 * r + 256 * j
            amp_out[:, at : at + 256] = amp_float.astype(BF16)
            like_out[:, at : at + 256] = like_float.astype(BF16)


def per_device(density, valid, row_taps, col_taps, amp_matrix, like_matrix):
    vmem = pl.BlockSpec(memory_space=pltpu.VMEM)
    anywhere = pl.BlockSpec(memory_space=pl.ANY)
    dma = pltpu.SemaphoreType.DMA
    blocks, weights = pl.pallas_call(
        exchange_kernel,
        out_shape=(
            jax.ShapeDtypeStruct((16, 2, 16, 1024), BF16),
            jax.ShapeDtypeStruct((1024, 512), BF16),
        ),
        in_specs=[vmem] * 6,
        out_specs=(anywhere, anywhere),
        scratch_shapes=[
            pltpu.VMEM((32, 256), F32),
            pltpu.VMEM((4, 4, 128, 256), BF16),
            pltpu.VMEM((4, 128, 1024), BF16),
            pltpu.VMEM((4, 256, 1024), BF16),
            pltpu.VMEM((4, 8, 32, 1024), BF16),
            pltpu.VMEM((4, 8, 32, 128), F32),
            pltpu.VMEM((16, 2, 16, 1024), BF16),
            pltpu.VMEM((8, 128), F32),
            pltpu.VMEM((16, 8, 128), F32),
            pltpu.VMEM((8, 128), F32),
            pltpu.VMEM((2, 4, 8, 1024), BF16),
            pltpu.VMEM((2, 4, 8, 1024), BF16),
            pltpu.VMEM((1024, 512), BF16),
            dma((16,)), dma((16,)), dma((2,)), dma((2,)),
            dma((16, 2)), dma((16, 2)), dma, dma,
        ],
        compiler_params=pltpu.CompilerParams(collective_id=0, has_side_effects=True),
        name="filter_exchange",
    )(density, valid, row_taps, col_taps, amp_matrix, like_matrix)
    out = jax.ShapeDtypeStruct((128, 4096), BF16)
    return pl.pallas_call(
        project_kernel,
        out_shape=(out, out),
        in_specs=[vmem] * 2,
        out_specs=(vmem, vmem),
        name="project",
    )(blocks.reshape(512, 1024), weights)


def solution(mesh):
    return jax.shard_map(
        per_device,
        mesh=mesh,
        in_specs=(
            P("cuts", "tile", None),
            P("tile", None),
            P(None, "cuts", None),
            P(None, "cuts", None),
            P(),
            P(),
        ),
        out_specs=(P(None, ("tile", "cuts")), P(None, ("tile", "cuts"))),
        check_vma=False,
    )
```

```python
import functools

import jax
import jax.numpy as jnp
from jax import lax
from jax.experimental import pallas as pl
from jax.experimental.pallas import tpu as pltpu
from jax.sharding import PartitionSpec as P

MESH = pl.DeviceIdType.MESH
REACH = 8
TAPS = 2 * REACH + 1
ABSENT = 1024.0
F32 = jnp.float32
BF16 = jnp.bfloat16


def distance(p):
    return (8 - (p + 1) // 2) * (2 * (p % 2) - 1)


def exchange_kernel(
    dens_in, valid_in, rtap, ctap, amp, like,
    recv, wout,
    dens, valid, base, rband, cband, field, wide, outs, send, stat, stats, bgs, hsend, hrecv, wmat,
    stat_ssem, stat_rsem, halo_ssem, halo_rsem, ssem, rsem, wsem, osem, vsem, dsem, up, down,
):
    n_s, n_row, n_col = dens.shape
    n_tile, n_cut = lax.axis_size("tile"), lax.axis_size("cuts")
    n_z = n_cut // 2
    tile, me = lax.axis_index("tile"), lax.axis_index("cuts")
    z, core = me // 2, me % 2
    n_a = n_col // 128

    loads = [pltpu.make_async_copy(valid_in, valid, vsem)]
    loads += [pltpu.make_async_copy(dens_in.at[s], dens.at[s], dsem.at[s]) for s in range(n_s)]
    for load in loads:
        load.start()

    barrier = pltpu.get_barrier_semaphore()
    for i in range(1, n_tile):
        pl.semaphore_signal(barrier, inc=1, device_id={"tile": (tile + i) % n_tile}, device_id_type=MESH)
    above, below = (z + 1) % n_z, (z + n_z - 1) % n_z
    near = (2 * above, 2 * above + 1, 2 * below, 2 * below + 1, 2 * z + 1 - core)
    for peer in near:
        pl.semaphore_signal(barrier, inc=1, device_id={"cuts": peer}, device_id_type=MESH)

    base[...] = jnp.zeros_like(base)
    for k in range(4):
        base[4 * k : 4 * k + 4, 0:TAPS] = rtap[k].astype(F32)
        base[16 + 4 * k : 20 + 4 * k, 0:TAPS] = ctap[k].astype(F32)
    base[...] = pltpu.roll(base[...], 256 - REACH, 1)
    for s in range(n_s):
        field[s, n_row : 2 * n_row, :] = jnp.zeros((n_row, n_col), BF16)

    for load in loads:
        load.wait()

    def fold(x):
        x = x[0:8] + x[8:16]
        total = x[:, 0:128]
        for a in range(1, n_a):
            total = total + x[:, 128 * a : 128 * a + 128]
        return total

    def sum_rows(i, accs):
        rows = pl.ds(pl.multiple_of(i * 16, 16), 16)
        mask = valid[rows, :].astype(F32)
        out = [accs[s] + fold(dens[s, rows, :].astype(F32) * mask) for s in range(n_s)]
        return (*out, accs[n_s] + fold(mask))

    accs = lax.fori_loop(0, n_row // 16, sum_rows, tuple(jnp.zeros((8, 128), F32) for _ in range(n_s + 1)))
    stat[...] = jnp.zeros_like(stat)
    for s in range(n_s + 1):
        stat[s : s + 1, :] = jnp.sum(accs[s], axis=0, keepdims=True)

    top, low = valid[0:8, :] != 0, valid[n_row - 8 : n_row, :] != 0
    for s in range(n_s):
        hsend[0, s] = jnp.where(top, dens[s, 0:16, :].astype(F32)[0:8], ABSENT).astype(BF16)
        hsend[1, s] = jnp.where(low, dens[s, n_row - 16 : n_row, :].astype(F32)[8:16], ABSENT).astype(BF16)

    pl.semaphore_wait(barrier, n_tile - 1 + len(near))

    stat_copies = []
    for i in range(1, n_tile):
        stat_copies.append(
            pltpu.make_async_remote_copy(
                stat, stats.at[i], stat_ssem.at[i], stat_rsem.at[i],
                device_id={"tile": (tile + i) % n_tile}, device_id_type=MESH,
            )
        )
    halo_copies = []
    for side, step in ((0, n_tile - 1), (1, 1)):
        halo_copies.append(
            pltpu.make_async_remote_copy(
                hsend.at[side], hrecv.at[side], halo_ssem.at[side], halo_rsem.at[side],
                device_id={"tile": (tile + step) % n_tile}, device_id_type=MESH,
            )
        )
    for copy in stat_copies + halo_copies:
        copy.start()

    def tell(d):
        pl.semaphore_signal(up.at[d - 2], inc=1, device_id={"cuts": 2 * above + core}, device_id_type=MESH)
        if d < n_z // 2:
            pl.semaphore_signal(down.at[d - 2], inc=1, device_id={"cuts": 2 * below + core}, device_id_type=MESH)

    def hear(d):
        pl.semaphore_wait(up.at[d - 2], 1)
        if d < n_z // 2:
            pl.semaphore_wait(down.at[d - 2], 1)

    def build(k):
        for s in range(n_s):
            row = jnp.broadcast_to(base[pl.ds(4 * k + s, 1), :], (8, 256))
            row = pltpu.roll(row, 0, 1, stride=1, stride_axis=0)
            if s % 2:
                row = pltpu.roll(row, 4, 0)
            for p in range(0, n_z, 2):
                pair = [pltpu.roll(row, 8 * ((z + distance(p + i) + n_z) % n_z), 1) for i in range(2)]
                rows = pl.ds(pl.multiple_of(32 * k + 8 * (p % 4), 16), 16)
                rband[s, p // 4, rows, :] = jnp.concatenate(pair, axis=0).astype(BF16)
            col = jnp.broadcast_to(base[pl.ds(16 + 4 * k + s, 1), :], (8, 256))
            col = pltpu.roll(col, 0, 1, stride=1, stride_axis=0)
            lanes = pl.ds(pl.multiple_of(256 * k, 256), 256)
            for m in range(0, 16, 2):
                pair = [pltpu.roll(col, 8 * (m + i), 1) if m + i else col for i in range(2)]
                cband[s, 8 * m : 8 * m + 16, lanes] = jnp.concatenate(pair, axis=0).astype(BF16)

    for d in range(2, 6):
        tell(d)
        build(d - 2)
        hear(d)
    tell(6)

    for copy in stat_copies:
        copy.wait()
    total = stat[...]
    for i in range(1, n_tile):
        total = total + stats[i]
    total = jnp.broadcast_to(jnp.sum(total, axis=1, keepdims=True), (8, 128))
    bgs[...] = total / jnp.broadcast_to(total[n_s : n_s + 1, :], (8, 128))

    def level(s):
        return jnp.concatenate([bgs[pl.ds(s, 1), :]] * n_a, axis=1)

    def mask_rows(i, carry):
        rows = pl.ds(pl.multiple_of(i * 16, 16), 16)
        mask = valid[rows, :].astype(F32)
        for s in range(n_s):
            field[s, rows, :] = (mask * (dens[s, rows, :].astype(F32) - level(s))).astype(BF16)
        return carry

    lax.fori_loop(0, n_row // 16, mask_rows, 0)
    hear(6)
    tell(7)
    for copy in halo_copies:
        copy.wait()
    has_after = (tile < n_tile - 1).astype(F32)
    has_before = (tile > 0).astype(F32)
    for s in range(n_s):
        after, before = hrecv[0, s].astype(F32), hrecv[1, s].astype(F32)
        after = jnp.where(after > 0.5 * ABSENT, 0.0, after - level(s)) * has_after
        before = jnp.where(before > 0.5 * ABSENT, 0.0, before - level(s)) * has_before
        none = jnp.zeros((8, n_col), F32)
        field[s, n_row : n_row + 16, :] = jnp.concatenate([after, none], axis=0).astype(BF16)
        field[s, 2 * n_row - 16 : 2 * n_row, :] = jnp.concatenate([none, before], axis=0).astype(BF16)

    def block_copy(p, c):
        target = 2 * ((z + distance(p) + n_z) % n_z) + c
        return pltpu.make_async_remote_copy(
            send.at[p, c], recv.at[p, core], ssem.at[p, c], rsem.at[p, core],
            device_id={"cuts": target}, device_id_type=MESH,
        )

    lane = lax.broadcasted_iota(jnp.int32, (32, 128), 1)
    first = lax.broadcasted_iota(jnp.int32, (8, 128), 0) < 4

    def filtered(q, s):
        rowed = jnp.dot(rband[s, q], field[s], preferred_element_type=F32)
        for k in range(4):
            tiles = [rowed[32 * k : 32 * k + 32, 128 * a : 128 * a + 128] for a in range(n_a)]
            for a in range(n_a):
                right = tiles[a + 1] if a + 1 < n_a else jnp.zeros((32, 128), F32)
                left = tiles[a - 1] if a else jnp.zeros((32, 128), F32)
                wide[s, a, :, 256 * k : 256 * k + 128] = tiles[a].astype(BF16)
                wide[s, a, :, 256 * k + 128 : 256 * k + 256] = jnp.where(lane < 64, right, left).astype(BF16)
        done = lax.dot_general(
            wide[s].reshape(32 * n_a, 1024), cband[s], (((1,), (1,)), ((), ())), preferred_element_type=F32
        )
        outs[s] = done.reshape(n_a, 32, 128)

    def pack(q):
        for i in range(4):
            p = 4 * q + i
            for a in range(n_a):
                part = [outs[s, a, 8 * i : 8 * i + 8, :] for s in range(n_s)]
                even = [jnp.where(first, part[0], part[1]), jnp.where(first, part[2], part[3])]
                odd = [jnp.where(first, part[1], part[0]), jnp.where(first, part[3], part[2])]
                send[p, 0, :, 128 * a : 128 * a + 128] = jnp.concatenate(even, axis=0).astype(BF16)
                send[p, 1, :, 128 * a : 128 * a + 128] = jnp.concatenate(odd, axis=0).astype(BF16)

    for s in range(n_s):
        filtered(0, s)
    pack(0)
    hear(7)
    tell(8)
    hear(8)
    for p in range(4):
        for c in range(2):
            block_copy(p, c).start()

    def chunk(q, carry):
        for s in range(n_s):
            filtered(q, s)
        pack(q)
        for i in range(4):
            for c in range(2):
                pl.when(jnp.logical_or(4 * q + i < 15, c != core))(block_copy(4 * q + i, c).start)
        return carry

    lax.fori_loop(1, n_z // 4, chunk, 0)
    own = pltpu.make_async_copy(send.at[15, core], recv.at[15, core], osem)
    own.start()

    both = jnp.concatenate([amp[...].astype(F32).T, like[...].astype(F32).T], axis=0).astype(BF16)
    at = lax.broadcasted_iota(jnp.int32, (8, 512), 1)
    pos = at >> 5
    dist = (8 - ((pos + 1) >> 1)) * (2 * (pos & 1) - 1)
    inner = (at >> 2) & 3
    inner = inner + core * (1 - 2 * (inner & 1))
    slices = 8 * ((z - dist + 2 * n_z) & (n_z - 1)) + 4 * ((at >> 4) & 1) + inner
    slices = jnp.concatenate([slices] * 16, axis=0)
    row_of = jnp.concatenate([at & 3] * 16, axis=0)
    wanted = slices == lax.broadcasted_iota(jnp.int32, (128, 512), 0)
    for r in range(4):
        pick = jnp.where(jnp.logical_and(wanted, row_of == r), 1.0, 0.0).astype(BF16)
        wmat[256 * r : 256 * r + 256, :] = jnp.dot(both, pick, preferred_element_type=F32).astype(BF16)
    put = pltpu.make_async_copy(wmat, wout, wsem)
    put.start()

    own.wait()
    put.wait()

    def finish(p, carry):
        for c in range(2):

            @pl.when(jnp.logical_or(p < 15, c != core))
            def _():
                block_copy(p, c).wait_send()
                pltpu.make_async_remote_copy(
                    send.at[p, c], recv.at[p, c], ssem.at[p, c], rsem.at[p, c],
                    device_id={"cuts": me}, device_id_type=MESH,
                ).wait_recv()

        return carry

    lax.fori_loop(0, n_z, finish, 0)


def project_kernel(blocks, weights, amp_out, like_out, amps, likes, sems):
    copies = []
    for j in range(4):
        part = blocks[:, :, :, 256 * j : 256 * j + 256].reshape(512, 256)
        both = jnp.dot(weights[...], part, preferred_element_type=F32)
        for r in range(4):
            amp_float = both[256 * r : 256 * r + 128]
            like_float = amp_float * both[256 * r + 128 : 256 * r + 256]
            at = pl.ds(1024 * r + 256 * j, 256)
            amps[:, at] = amp_float.astype(BF16)
            likes[:, at] = like_float.astype(BF16)
            for i, (kept, out) in enumerate(((amps, amp_out), (likes, like_out))):
                copy = pltpu.make_async_copy(kept.at[:, at], out.at[:, at], sems.at[i, j, r])
                copy.start()
                copies.append(copy)
    for copy in copies:
        copy.wait()


def per_device(density, valid, row_taps, col_taps, amp_matrix, like_matrix):
    vmem = pl.BlockSpec(memory_space=pltpu.VMEM)
    anywhere = pl.BlockSpec(memory_space=pl.ANY)
    dma = pltpu.SemaphoreType.DMA
    blocks, weights = pl.pallas_call(
        exchange_kernel,
        out_shape=(
            pltpu.VMEM((16, 2, 16, 1024), BF16),
            pltpu.VMEM((1024, 512), BF16),
        ),
        in_specs=[anywhere] * 2 + [vmem] * 4,
        out_specs=(vmem, vmem),
        scratch_shapes=[
            pltpu.VMEM((4, 128, 1024), BF16),
            pltpu.VMEM((128, 1024), jnp.int32),
            pltpu.VMEM((32, 256), F32),
            pltpu.VMEM((4, 4, 128, 256), BF16),
            pltpu.VMEM((4, 128, 1024), BF16),
            pltpu.VMEM((4, 256, 1024), BF16),
            pltpu.VMEM((4, 8, 32, 1024), BF16),
            pltpu.VMEM((4, 8, 32, 128), F32),
            pltpu.VMEM((16, 2, 16, 1024), BF16),
            pltpu.VMEM((8, 128), F32),
            pltpu.VMEM((16, 8, 128), F32),
            pltpu.VMEM((8, 128), F32),
            pltpu.VMEM((2, 4, 8, 1024), BF16),
            pltpu.VMEM((2, 4, 8, 1024), BF16),
            pltpu.VMEM((1024, 512), BF16),
            dma((16,)), dma((16,)), dma((2,)), dma((2,)),
            dma((16, 2)), dma((16, 2)), dma, dma, dma, dma((4,)),
            pltpu.SemaphoreType.REGULAR((8,)), pltpu.SemaphoreType.REGULAR((8,)),
        ],
        compiler_params=pltpu.CompilerParams(collective_id=0, has_side_effects=True),
        name="filter_exchange",
    )(density, valid, row_taps, col_taps, amp_matrix, like_matrix)
    out = jax.ShapeDtypeStruct((128, 4096), BF16)
    return pl.pallas_call(
        project_kernel,
        out_shape=(out, out),
        in_specs=[vmem] * 2,
        out_specs=(anywhere, anywhere),
        scratch_shapes=[pltpu.VMEM((128, 4096), BF16), pltpu.VMEM((128, 4096), BF16), dma((2, 4, 4))],
        name="project",
    )(
        pltpu.with_memory_space_constraint(blocks, pltpu.VMEM),
        pltpu.with_memory_space_constraint(weights, pltpu.VMEM),
    )


def solution(mesh):
    return jax.shard_map(
        per_device,
        mesh=mesh,
        in_specs=(
            P("cuts", "tile", None),
            P("tile", None),
            P(None, "cuts", None),
            P(None, "cuts", None),
            P(),
            P(),
        ),
        out_specs=(P(None, ("tile", "cuts")), P(None, ("tile", "cuts"))),
        check_vma=False,
    )
```

```python
import functools

import jax
import jax.numpy as jnp
from jax import lax
from jax.experimental import pallas as pl
from jax.experimental.pallas import tpu as pltpu
from jax.sharding import PartitionSpec as P

MESH = pl.DeviceIdType.MESH
REACH = 8
TAPS = 2 * REACH + 1
ABSENT = 1024.0
F32 = jnp.float32
BF16 = jnp.bfloat16

ORDER = (7, -7, 6, -6, 8, 5, -5, 4, -4, 3, -3, 2, -2, 1, -1, 0)
EARLY = 4
SELF = 15


def distance(p):
    return ORDER[p]


def exchange_kernel(
    dens_in, valid_in, rtap_in, ctap_in, amp_in, like_in,
    recv, wmat, acc,
    dens, valid, rtap, ctap, amp, like, base, rband, cband, field, wide, outs, send, stat, stats, bgs, hsend, hrecv,
    raw, local, delta, msg, msgs, seen, shifted, gmat,
    stat_ssem, stat_rsem, halo_ssem, halo_rsem, ssem, rsem, osem, vsem, dsem, small_sem, row_in, col_in, msg_ssem, msg_rsem,
):
    n_s, n_row, n_col = dens.shape
    n_tile, n_cut = lax.axis_size("tile"), lax.axis_size("cuts")
    n_z = n_cut // 2
    tile, me = lax.axis_index("tile"), lax.axis_index("cuts")
    z, core = me // 2, me % 2
    n_a = n_col // 128

    loads = [pltpu.make_async_copy(valid_in, valid, vsem)]
    loads += [pltpu.make_async_copy(dens_in.at[s], dens.at[s], dsem.at[s]) for s in range(n_s)]
    small = [(rtap_in, rtap), (ctap_in, ctap), (amp_in, amp), (like_in, like)]
    small = [pltpu.make_async_copy(a, b, small_sem.at[i]) for i, (a, b) in enumerate(small)]
    for load in small[:2] + loads + small[2:]:
        load.start()

    barrier = pltpu.get_barrier_semaphore()
    n_x = 4
    n_y = n_tile // n_x
    y, x = tile // n_x, tile % n_x
    left, right = n_x * y + (x + n_x - 1) % n_x, n_x * y + (x + 1) % n_x
    back, front = n_x * ((y + n_y - 1) % n_y) + x, n_x * ((y + 1) % n_y) + x
    def signal_tile(sem, peer):
        pl.semaphore_signal(sem, inc=1, device_id={"tile": peer}, device_id_type=MESH)

    for i in range(n_z // 2, -1, -1):
        for peer_z in (z + i, z + n_z - i)[: 1 if i % (n_z // 2) == 0 else 2]:
            for c in range(2 if i else 1):
                peer = 2 * (peer_z % n_z) + (c if i else 1 - core)
                pl.semaphore_signal(barrier, inc=1, device_id={"cuts": peer}, device_id_type=MESH)
    for peer in (left, right, back, front):
        signal_tile(barrier, peer)
    not_first, not_last = tile > 0, tile < n_tile - 1

    @pl.when(not_first)
    def _():
        signal_tile(barrier, tile - 1)

    @pl.when(not_last)
    def _():
        signal_tile(barrier, tile + 1)

    for load in small[:2]:
        load.wait()
    raw[...] = jnp.zeros_like(raw)
    for k in range(4):
        raw[4 * k : 4 * k + 4, 0:TAPS] = rtap[k].astype(F32)
        raw[16 + 4 * k : 20 + 4 * k, 0:TAPS] = ctap[k].astype(F32)
    base[...] = pltpu.roll(jnp.concatenate([raw[...], jnp.zeros_like(raw)], axis=1), 256 - REACH, 1)
    for s in range(n_s):
        field[s, n_row : 2 * n_row, :] = jnp.zeros((n_row, n_col), BF16)

    for load in loads:
        load.wait()

    def fold(x):
        x = x[0:8] + x[8:16]
        total = x[:, 0:128]
        for a in range(1, n_a):
            total = total + x[:, 128 * a : 128 * a + 128]
        return total

    def sum_rows(i, accs):
        rows = pl.ds(pl.multiple_of(i * 16, 16), 16)
        mask = valid[rows, :].astype(F32)
        out = [accs[s] + fold(dens[s, rows, :].astype(F32) * mask) for s in range(n_s)]
        return (*out, accs[n_s] + fold(mask))

    accs = lax.fori_loop(0, n_row // 16, sum_rows, tuple(jnp.zeros((8, 128), F32) for _ in range(n_s + 1)))
    stat[...] = jnp.zeros_like(stat)
    for s in range(n_s + 1):
        stat[s : s + 1, :] = jnp.sum(accs[s], axis=0, keepdims=True)

    def mean(total):
        total = jnp.broadcast_to(jnp.sum(total, axis=1, keepdims=True), (8, 128))
        return total / jnp.broadcast_to(total[n_s : n_s + 1, :], (8, 128))

    local[...] = mean(stat[...])

    top, low = valid[0:8, :] != 0, valid[n_row - 8 : n_row, :] != 0
    for s in range(n_s):
        hsend[0, s] = jnp.where(top, dens[s, 0:16, :].astype(F32)[0:8], ABSENT).astype(BF16)
        hsend[1, s] = jnp.where(low, dens[s, n_row - 16 : n_row, :].astype(F32)[8:16], ABSENT).astype(BF16)

    def build(k):
        for s in range(n_s):
            row = jnp.broadcast_to(base[pl.ds(4 * k + s, 1), :], (8, 256))
            row = pltpu.roll(row, 0, 1, stride=1, stride_axis=0)
            if s % 2:
                row = pltpu.roll(row, 4, 0)
            for p in range(0, n_z, 2):
                pair = [pltpu.roll(row, 8 * ((z + distance(p + i) + n_z) % n_z), 1) for i in range(2)]
                rows = pl.ds(pl.multiple_of(32 * k + 8 * (p % 4), 16), 16)
                rband[s, p // 4, rows, :] = jnp.concatenate(pair, axis=0).astype(BF16)
            col = jnp.broadcast_to(base[pl.ds(16 + 4 * k + s, 1), :], (8, 256))
            col = pltpu.roll(col, 0, 1, stride=1, stride_axis=0)
            lanes = pl.ds(pl.multiple_of(256 * k, 256), 256)
            for m in range(0, 16, 2):
                pair = [pltpu.roll(col, 8 * (m + i), 1) if m + i else col for i in range(2)]
                cband[s, 8 * m : 8 * m + 16, lanes] = jnp.concatenate(pair, axis=0).astype(BF16)

    for k in range(4):
        build(k)

    @pl.when(jnp.logical_not(not_last))
    def _():
        hrecv[0] = jnp.full((n_s, 8, n_col), ABSENT, BF16)

    @pl.when(jnp.logical_not(not_first))
    def _():
        hrecv[1] = jnp.full((n_s, 8, n_col), ABSENT, BF16)

    def fill_field(levels):
        def level(s):
            return jnp.concatenate([levels[pl.ds(s, 1), :]] * n_a, axis=1)

        def mask_rows(i, carry):
            rows = pl.ds(pl.multiple_of(i * 16, 16), 16)
            mask = valid[rows, :].astype(F32)
            for s in range(n_s):
                field[s, rows, :] = (mask * (dens[s, rows, :].astype(F32) - level(s))).astype(BF16)
            return carry

        lax.fori_loop(0, n_row // 16, mask_rows, 0)
        return level

    def fill_halo(level):
        for s in range(n_s):
            after, before = hrecv[0, s].astype(F32), hrecv[1, s].astype(F32)
            after = jnp.where(after > 0.5 * ABSENT, 0.0, after - level(s))
            before = jnp.where(before > 0.5 * ABSENT, 0.0, before - level(s))
            none = jnp.zeros((8, n_col), F32)
            field[s, n_row : n_row + 16, :] = jnp.concatenate([after, none], axis=0).astype(BF16)
            field[s, 2 * n_row - 16 : 2 * n_row, :] = jnp.concatenate([none, before], axis=0).astype(BF16)

    level = fill_field(local)

    def block_copy(p, c):
        target = 2 * ((z + distance(p) + n_z) % n_z) + c
        return pltpu.make_async_remote_copy(
            send.at[p, c], recv.at[p, core], ssem.at[p, c], rsem.at[p, core],
            device_id={"cuts": target}, device_id_type=MESH,
        )

    lane = lax.broadcasted_iota(jnp.int32, (32, 128), 1)
    first = lax.broadcasted_iota(jnp.int32, (8, 128), 0) < 4

    def filtered(q, s):
        rowed = jnp.dot(rband[s, q], field[s], preferred_element_type=F32)
        for k in range(4):
            tiles = [rowed[32 * k : 32 * k + 32, 128 * a : 128 * a + 128] for a in range(n_a)]
            for a in range(n_a):
                right = tiles[a + 1] if a + 1 < n_a else jnp.zeros((32, 128), F32)
                left = tiles[a - 1] if a else jnp.zeros((32, 128), F32)
                wide[s, a, :, 256 * k : 256 * k + 128] = tiles[a].astype(BF16)
                wide[s, a, :, 256 * k + 128 : 256 * k + 256] = jnp.where(lane < 64, right, left).astype(BF16)
        done = lax.dot_general(
            wide[s].reshape(32 * n_a, 1024), cband[s], (((1,), (1,)), ((), ())), preferred_element_type=F32
        )
        outs[s] = done.reshape(n_a, 32, 128)

    def pack_one(p):
        i = p % 4
        for a in range(n_a):
            part = [outs[s, a, 8 * i : 8 * i + 8, :] for s in range(n_s)]
            even = [jnp.where(first, part[0], part[1]), jnp.where(first, part[2], part[3])]
            odd = [jnp.where(first, part[1], part[0]), jnp.where(first, part[3], part[2])]
            send[p, 0, :, 128 * a : 128 * a + 128] = jnp.concatenate(even, axis=0).astype(BF16)
            send[p, 1, :, 128 * a : 128 * a + 128] = jnp.concatenate(odd, axis=0).astype(BF16)

    def start_one(p):
        for c in range(2):
            if p == SELF:
                pl.when(c != core)(block_copy(p, c).start)
            else:
                block_copy(p, c).start()

    def at_edge(p):
        target = (z + distance(p) + n_z) % n_z
        return jnp.logical_or(target == 0, target == n_z - 1)

    for s in range(n_s):
        filtered(0, s)
    for p in range(EARLY):
        pl.when(jnp.logical_not(at_edge(p)))(functools.partial(pack_one, p))

    pl.semaphore_wait(barrier, 4 + n_cut - 1 + not_first.astype(jnp.int32) + not_last.astype(jnp.int32))

    def halo_copy(side, peer):
        return pltpu.make_async_remote_copy(
            hsend.at[side], hrecv.at[side], halo_ssem.at[side], halo_rsem.at[side],
            device_id={"tile": peer}, device_id_type=MESH,
        )

    pl.when(not_first)(lambda: halo_copy(0, tile - 1).start())
    pl.when(not_last)(lambda: halo_copy(1, tile + 1).start())

    for p in range(EARLY):
        pl.when(jnp.logical_not(at_edge(p)))(functools.partial(start_one, p))

    @pl.when(not_first)
    def _():
        halo_copy(0, tile - 1).wait_send()
        halo_copy(1, tile - 1).wait_recv()

    @pl.when(not_last)
    def _():
        halo_copy(1, tile + 1).wait_send()
        halo_copy(0, tile + 1).wait_recv()

    fill_halo(level)
    for s in range(n_s):
        filtered(0, s)
    for p in range(EARLY):

        @pl.when(at_edge(p))
        def _():
            pack_one(p)
            start_one(p)

    stat_copies = []
    for i in range(1, n_tile):
        stat_copies.append(
            pltpu.make_async_remote_copy(
                stat, stats.at[i], stat_ssem.at[i], stat_rsem.at[i],
                device_id={"tile": (tile + i) % n_tile}, device_id_type=MESH,
            )
        )

    signal_tile(row_in, right)
    pl.semaphore_wait(row_in, 1)
    signal_tile(col_in.at[0], front)
    signal_tile(col_in.at[1], back)
    pl.semaphore_wait(col_in.at[0], 1)
    pl.semaphore_wait(col_in.at[1], 1)
    signal_tile(col_in.at[2], front)
    pl.semaphore_wait(col_in.at[2], 1)
    for copy in stat_copies:
        copy.start()

    for copy in stat_copies:
        copy.wait()
    total = stat[...]
    for i in range(1, n_tile):
        total = total + stats[i]
    bgs[...] = mean(total)
    delta[...] = bgs[...] - local[...]
    off = delta[0:4, :]
    parts = []
    for k in range(2):
        r, c = 8 * k, 16 + 8 * k
        part = raw[c : c + 4, :] + pltpu.roll(raw[r : r + 4, :] * off, 32, 1)
        part = part + pltpu.roll(raw[c + 4 : c + 8, :], 64, 1) + pltpu.roll(raw[r + 4 : r + 8, :] * off, 96, 1)
        parts.append(part)
    msg[...] = jnp.concatenate(parts, axis=0).astype(BF16)

    def msg_copy(p, c):
        target = 2 * ((z + distance(p) + n_z) % n_z) + c
        return pltpu.make_async_remote_copy(
            msg, msgs.at[p, core], msg_ssem.at[p, c], msg_rsem.at[p, core],
            device_id={"cuts": target}, device_id_type=MESH,
        )

    for p in range(EARLY):
        for c in range(2):
            msg_copy(p, c).start()

    level = fill_field(bgs)
    fill_halo(level)
    for q in range(1, n_z // 4):
        for s in range(n_s):
            filtered(q, s)
        for p in range(4 * q, 4 * q + 4):
            pack_one(p)
        for p in range(4 * q, 4 * q + 4):
            start_one(p)

    own = pltpu.make_async_copy(send.at[15, core], recv.at[15, core], osem)
    own.start()

    for load in small[2:]:
        load.wait()

    both = jnp.concatenate([amp[...].astype(F32).T, like[...].astype(F32).T], axis=0).astype(BF16)
    at = lax.broadcasted_iota(jnp.int32, (8, 512), 1)

    def tall(x):
        return jnp.concatenate([x] * 16, axis=0)

    def source_slice(pos, source_core, inner):
        dist = jnp.zeros_like(pos)
        for p in range(n_z):
            dist = jnp.where(pos == p, ORDER[p], dist)
        return 8 * ((z - dist + 2 * n_z) & (n_z - 1)) + 4 * source_core + inner

    inner = (at >> 2) & 3
    inner = inner + core * (1 - 2 * (inner & 1))
    slices = tall(source_slice(at >> 5, (at >> 4) & 1, inner))
    row_of = tall(at & 3)
    down_at = lax.broadcasted_iota(jnp.int32, (128, 512), 0)
    for r in range(4):
        pick = jnp.where(jnp.logical_and(slices == down_at, row_of == r), 1.0, 0.0).astype(BF16)
        wmat[256 * r : 256 * r + 256, :] = jnp.dot(both, pick, preferred_element_type=F32).astype(BF16)

    for i in range(2):
        absent = hrecv[i, 0].astype(F32) > 0.5 * ABSENT
        seen[n_row + 8 if i == 0 else 0 : n_row + 16 if i == 0 else 8, :] = (
            jnp.where(absent, 0.0, 1.0)
        )
    seen[8 : n_row + 8, :] = valid[...].astype(F32)
    seen[n_row + 16 : n_row + 24, :] = jnp.zeros((8, n_col), F32)
    window = seen[pl.ds(pl.multiple_of(8 * z, 8), 32), :]
    window = jnp.where(core == 0, window[0:24], pltpu.roll(window, 28, 0)[0:24])
    window = jnp.concatenate([window, jnp.zeros((24, 128), F32)], axis=1)
    for j in range(TAPS):
        turned = pltpu.roll(window, (REACH - j) % (n_col + 128), 1) if j != REACH else window
        shifted[24 * j : 24 * j + 24, :] = turned[:, 0:n_col]
    shifted[24 * TAPS : 512, :] = jnp.zeros((512 - 24 * TAPS, n_col), F32)

    for p in range(EARLY):
        for c in range(2):
            msg_copy(p, c).wait_send()
            pltpu.make_async_remote_copy(
                msg, msgs.at[p, c], msg_ssem.at[p, c], msg_rsem.at[p, c],
                device_id={"cuts": me}, device_id_type=MESH,
            ).wait_recv()

    column = jnp.zeros_like(at)
    for j in range(1, 22):
        column = column + jnp.where(at >= 24 * j, 1, 0)
    row = at - 24 * column
    column, row = tall(column), tall(row)
    terms = msgs[...].reshape(64, 128)

    def spread(lane_of):
        return jnp.dot(terms, jnp.where(down_at == lane_of, 1.0, 0.0).astype(BF16), preferred_element_type=F32)

    at = lax.broadcasted_iota(jnp.int32, (128, 64), 1)
    wanted = source_slice(at >> 4, (at >> 3) & 1, at & 3) == lax.broadcasted_iota(jnp.int32, (128, 64), 0)
    mixed = jnp.dot(both, jnp.where(wanted, 1.0, 0.0).astype(BF16), preferred_element_type=F32).astype(BF16)
    col_terms = [spread(column + 64 * k) for k in range(2)]
    for r in range(4):
        product = col_terms[0] * spread(32 + row - r) + col_terms[1] * spread(96 + row - r)
        gmat[256 * r : 256 * r + 256, :] = -jnp.dot(mixed, product.astype(BF16), preferred_element_type=F32)

    def correct(j, carry):
        lanes = pl.ds(pl.multiple_of(256 * j, 256), 256)
        acc[:, lanes] = jnp.dot(gmat[...].astype(BF16), shifted[:, lanes].astype(BF16), preferred_element_type=F32)
        return carry

    lax.fori_loop(0, n_col // 256, correct, 0)

    own.wait()
    for p in range(n_z):
        for c in range(2):

            def finish():
                block_copy(p, c).wait_send()
                pltpu.make_async_remote_copy(
                    send.at[p, c], recv.at[p, c], ssem.at[p, c], rsem.at[p, c],
                    device_id={"cuts": me}, device_id_type=MESH,
                ).wait_recv()

            if p == SELF:
                pl.when(c != core)(finish)
            else:
                finish()


def project_kernel(blocks, weights, acc, amp_out, like_out, amps, likes, sems):
    copies = []
    for j in range(4):
        part = blocks[:, :, :, 256 * j : 256 * j + 256].reshape(512, 256)
        both = jnp.dot(weights[...], part, preferred_element_type=F32) + acc[:, 256 * j : 256 * j + 256]
        for r in range(4):
            amp_float = both[256 * r : 256 * r + 128]
            like_float = amp_float * both[256 * r + 128 : 256 * r + 256]
            at = pl.ds(1024 * r + 256 * j, 256)
            amps[:, at] = amp_float.astype(BF16)
            likes[:, at] = like_float.astype(BF16)
            for i, (kept, out) in enumerate(((amps, amp_out), (likes, like_out))):
                copy = pltpu.make_async_copy(kept.at[:, at], out.at[:, at], sems.at[i, j, r])
                copy.start()
                copies.append(copy)
    for copy in copies:
        copy.wait()


def per_device(density, valid, row_taps, col_taps, amp_matrix, like_matrix):
    vmem = pl.BlockSpec(memory_space=pltpu.VMEM)
    anywhere = pl.BlockSpec(memory_space=pl.ANY)
    dma = pltpu.SemaphoreType.DMA
    blocks, weights, acc = pl.pallas_call(
        exchange_kernel,
        out_shape=(
            pltpu.VMEM((16, 2, 16, 1024), BF16),
            pltpu.VMEM((1024, 512), BF16),
            pltpu.VMEM((1024, 1024), F32),
        ),
        in_specs=[pl.BlockSpec(memory_space=pltpu.HBM)] * 6,
        out_specs=(vmem, vmem, vmem),
        scratch_shapes=[
            pltpu.VMEM((4, 128, 1024), BF16),
            pltpu.VMEM((128, 1024), jnp.int32),
            pltpu.VMEM((4, 4, 17), BF16),
            pltpu.VMEM((4, 4, 17), BF16),
            pltpu.VMEM((128, 128), BF16),
            pltpu.VMEM((128, 128), BF16),
            pltpu.VMEM((32, 256), F32),
            pltpu.VMEM((4, 4, 128, 256), BF16),
            pltpu.VMEM((4, 128, 1024), BF16),
            pltpu.VMEM((4, 256, 1024), BF16),
            pltpu.VMEM((4, 8, 32, 1024), BF16),
            pltpu.VMEM((4, 8, 32, 128), F32),
            pltpu.VMEM((16, 2, 16, 1024), BF16),
            pltpu.VMEM((8, 128), F32),
            pltpu.VMEM((16, 8, 128), F32),
            pltpu.VMEM((8, 128), F32),
            pltpu.VMEM((2, 4, 8, 1024), BF16),
            pltpu.VMEM((2, 4, 8, 1024), BF16),
            pltpu.VMEM((32, 128), F32),
            pltpu.VMEM((8, 128), F32),
            pltpu.VMEM((8, 128), F32),
            pltpu.VMEM((8, 128), BF16),
            pltpu.VMEM((EARLY, 2, 8, 128), BF16),
            pltpu.VMEM((152, 1024), F32),
            pltpu.VMEM((512, 1024), F32),
            pltpu.VMEM((1024, 512), F32),
            dma((16,)), dma((16,)), dma((2,)), dma((2,)),
            dma((16, 2)), dma((16, 2)), dma, dma, dma((4,)), dma((4,)),
            pltpu.SemaphoreType.REGULAR, pltpu.SemaphoreType.REGULAR((3,)),
            dma((EARLY, 2)), dma((EARLY, 2)),
        ],
        compiler_params=pltpu.CompilerParams(
            collective_id=0, has_side_effects=True, vmem_limit_bytes=44 * 1024 * 1024
        ),
        name="filter_exchange",
    )(*(
        pltpu.with_memory_space_constraint(x, pltpu.HBM)
        for x in (density, valid, row_taps, col_taps, amp_matrix, like_matrix)
    ))
    out = jax.ShapeDtypeStruct((128, 4096), BF16)
    return pl.pallas_call(
        project_kernel,
        out_shape=(out, out),
        in_specs=[vmem] * 3,
        out_specs=(anywhere, anywhere),
        scratch_shapes=[pltpu.VMEM((128, 4096), BF16), pltpu.VMEM((128, 4096), BF16), dma((2, 4, 4))],
        compiler_params=pltpu.CompilerParams(vmem_limit_bytes=44 * 1024 * 1024),
        name="project",
    )(
        pltpu.with_memory_space_constraint(blocks, pltpu.VMEM),
        pltpu.with_memory_space_constraint(weights, pltpu.VMEM),
        pltpu.with_memory_space_constraint(acc, pltpu.VMEM),
    )


def solution(mesh):
    return jax.shard_map(
        per_device,
        mesh=mesh,
        in_specs=(
            P("cuts", "tile", None),
            P("tile", None),
            P(None, "cuts", None),
            P(None, "cuts", None),
            P(),
            P(),
        ),
        out_specs=(P(None, ("tile", "cuts")), P(None, ("tile", "cuts"))),
        check_vma=False,
    )
```

```python
import functools

import jax
import jax.numpy as jnp
from jax import lax
from jax.experimental import pallas as pl
from jax.experimental.pallas import tpu as pltpu
from jax.sharding import PartitionSpec as P

MESH = pl.DeviceIdType.MESH
REACH = 8
TAPS = 2 * REACH + 1
ABSENT = 1024.0
F32 = jnp.float32
BF16 = jnp.bfloat16

ORDER = (7, -7, 6, -6, 8, 5, -5, 4, -4, 3, -3, 2, -2, 1, -1, 0)
EARLY = 4
SELF = 15


def distance(p):
    return ORDER[p]


def exchange_kernel(
    dens_in, valid_in, rtap_in, ctap_in, amp_in, like_in,
    recv, wmat, acc,
    dens, valid, rtap, ctap, amp, like, base, rband, cband, field, wide, outs, send, stat, stats, bgs, hsend, hrecv,
    raw, local, delta, msg, msgs, seen, shifted, gmat,
    stat_ssem, stat_rsem, halo_ssem, halo_rsem, ssem, rsem, osem, vsem, dsem, small_sem, row_in, col_in, msg_ssem, msg_rsem,
):
    n_s, n_row, n_col = dens.shape
    n_tile, n_cut = lax.axis_size("tile"), lax.axis_size("cuts")
    n_z = n_cut // 2
    tile, me = lax.axis_index("tile"), lax.axis_index("cuts")
    z, core = me // 2, me % 2
    n_a = n_col // 128

    loads = [pltpu.make_async_copy(valid_in, valid, vsem)]
    loads += [pltpu.make_async_copy(dens_in.at[s], dens.at[s], dsem.at[s]) for s in range(n_s)]
    small = [(rtap_in, rtap), (ctap_in, ctap), (amp_in, amp), (like_in, like)]
    small = [pltpu.make_async_copy(a, b, small_sem.at[i]) for i, (a, b) in enumerate(small)]
    for load in small[:2] + loads + small[2:]:
        load.start()

    barrier = pltpu.get_barrier_semaphore()
    n_x = 4
    n_y = n_tile // n_x
    y, x = tile // n_x, tile % n_x
    left, right = n_x * y + (x + n_x - 1) % n_x, n_x * y + (x + 1) % n_x
    back, front = n_x * ((y + n_y - 1) % n_y) + x, n_x * ((y + 1) % n_y) + x
    def signal_tile(sem, peer):
        pl.semaphore_signal(sem, inc=1, device_id={"tile": peer}, device_id_type=MESH)

    for i in range(n_z // 2, -1, -1):
        for peer_z in (z + i, z + n_z - i)[: 1 if i % (n_z // 2) == 0 else 2]:
            for c in range(2 if i else 1):
                peer = 2 * (peer_z % n_z) + (c if i else 1 - core)
                pl.semaphore_signal(barrier, inc=1, device_id={"cuts": peer}, device_id_type=MESH)
    for peer in (left, right, back, front):
        signal_tile(barrier, peer)
    not_first, not_last = tile > 0, tile < n_tile - 1

    @pl.when(not_first)
    def _():
        signal_tile(barrier, tile - 1)

    @pl.when(not_last)
    def _():
        signal_tile(barrier, tile + 1)

    for load in small[:2]:
        load.wait()
    raw[...] = jnp.zeros_like(raw)
    for k in range(4):
        raw[4 * k : 4 * k + 4, 0:TAPS] = rtap[k].astype(F32)
        raw[16 + 4 * k : 20 + 4 * k, 0:TAPS] = ctap[k].astype(F32)
    base[...] = pltpu.roll(jnp.concatenate([raw[...], jnp.zeros_like(raw)], axis=1), 256 - REACH, 1)
    for s in range(n_s):
        field[s, n_row : 2 * n_row, :] = jnp.zeros((n_row, n_col), BF16)

    for load in loads:
        load.wait()

    def fold(x):
        x = x[0:8] + x[8:16]
        total = x[:, 0:128]
        for a in range(1, n_a):
            total = total + x[:, 128 * a : 128 * a + 128]
        return total

    def sum_rows(i, accs):
        rows = pl.ds(pl.multiple_of(i * 16, 16), 16)
        mask = valid[rows, :].astype(F32)
        out = [accs[s] + fold(dens[s, rows, :].astype(F32) * mask) for s in range(n_s)]
        return (*out, accs[n_s] + fold(mask))

    accs = lax.fori_loop(0, n_row // 16, sum_rows, tuple(jnp.zeros((8, 128), F32) for _ in range(n_s + 1)))
    stat[...] = jnp.zeros_like(stat)
    for s in range(n_s + 1):
        stat[s : s + 1, :] = jnp.sum(accs[s], axis=0, keepdims=True)

    def mean(total):
        total = jnp.broadcast_to(jnp.sum(total, axis=1, keepdims=True), (8, 128))
        return total / jnp.broadcast_to(total[n_s : n_s + 1, :], (8, 128))

    local[...] = mean(stat[...])

    top, low = valid[0:8, :] != 0, valid[n_row - 8 : n_row, :] != 0
    for s in range(n_s):
        hsend[0, s] = jnp.where(top, dens[s, 0:16, :].astype(F32)[0:8], ABSENT).astype(BF16)
        hsend[1, s] = jnp.where(low, dens[s, n_row - 16 : n_row, :].astype(F32)[8:16], ABSENT).astype(BF16)

    def build(k):
        for s in range(n_s):
            row = jnp.broadcast_to(base[pl.ds(4 * k + s, 1), :], (8, 256))
            row = pltpu.roll(row, 0, 1, stride=1, stride_axis=0)
            if s % 2:
                row = pltpu.roll(row, 4, 0)
            for p in range(0, n_z, 2):
                pair = [pltpu.roll(row, 8 * ((z + distance(p + i) + n_z) % n_z), 1) for i in range(2)]
                rows = pl.ds(pl.multiple_of(32 * k + 8 * (p % 4), 16), 16)
                rband[s, p // 4, rows, :] = jnp.concatenate(pair, axis=0).astype(BF16)
            col = jnp.broadcast_to(base[pl.ds(16 + 4 * k + s, 1), :], (8, 256))
            col = pltpu.roll(col, 0, 1, stride=1, stride_axis=0)
            lanes = pl.ds(pl.multiple_of(256 * k, 256), 256)
            for m in range(0, 16, 2):
                pair = [pltpu.roll(col, 8 * (m + i), 1) if m + i else col for i in range(2)]
                cband[s, 8 * m : 8 * m + 16, lanes] = jnp.concatenate(pair, axis=0).astype(BF16)

    for k in range(4):
        build(k)

    @pl.when(jnp.logical_not(not_last))
    def _():
        hrecv[0] = jnp.full((n_s, 8, n_col), ABSENT, BF16)

    @pl.when(jnp.logical_not(not_first))
    def _():
        hrecv[1] = jnp.full((n_s, 8, n_col), ABSENT, BF16)

    def fill_field(levels):
        def level(s):
            return jnp.concatenate([levels[pl.ds(s, 1), :]] * n_a, axis=1)

        def mask_rows(i, carry):
            rows = pl.ds(pl.multiple_of(i * 16, 16), 16)
            mask = valid[rows, :].astype(F32)
            for s in range(n_s):
                field[s, rows, :] = (mask * (dens[s, rows, :].astype(F32) - level(s))).astype(BF16)
            return carry

        lax.fori_loop(0, n_row // 16, mask_rows, 0)
        return level

    def fill_halo(level):
        for s in range(n_s):
            after, before = hrecv[0, s].astype(F32), hrecv[1, s].astype(F32)
            after = jnp.where(after > 0.5 * ABSENT, 0.0, after - level(s))
            before = jnp.where(before > 0.5 * ABSENT, 0.0, before - level(s))
            none = jnp.zeros((8, n_col), F32)
            field[s, n_row : n_row + 16, :] = jnp.concatenate([after, none], axis=0).astype(BF16)
            field[s, 2 * n_row - 16 : 2 * n_row, :] = jnp.concatenate([none, before], axis=0).astype(BF16)

    level = fill_field(local)

    def block_copy(p, c):
        target = 2 * ((z + distance(p) + n_z) % n_z) + c
        return pltpu.make_async_remote_copy(
            send.at[p, c], recv.at[p, core], ssem.at[p, c], rsem.at[p, core],
            device_id={"cuts": target}, device_id_type=MESH,
        )

    lane = lax.broadcasted_iota(jnp.int32, (32, 128), 1)
    first = lax.broadcasted_iota(jnp.int32, (8, 128), 0) < 4

    def filtered(q, s):
        rowed = jnp.dot(rband[s, q], field[s], preferred_element_type=F32)
        for k in range(4):
            tiles = [rowed[32 * k : 32 * k + 32, 128 * a : 128 * a + 128] for a in range(n_a)]
            for a in range(n_a):
                right = tiles[a + 1] if a + 1 < n_a else jnp.zeros((32, 128), F32)
                left = tiles[a - 1] if a else jnp.zeros((32, 128), F32)
                wide[s, a, :, 256 * k : 256 * k + 128] = tiles[a].astype(BF16)
                wide[s, a, :, 256 * k + 128 : 256 * k + 256] = jnp.where(lane < 64, right, left).astype(BF16)
        done = lax.dot_general(
            wide[s].reshape(32 * n_a, 1024), cband[s], (((1,), (1,)), ((), ())), preferred_element_type=F32
        )
        outs[s] = done.reshape(n_a, 32, 128)

    def pack_one(p):
        i = p % 4
        for a in range(n_a):
            part = [outs[s, a, 8 * i : 8 * i + 8, :] for s in range(n_s)]
            even = [jnp.where(first, part[0], part[1]), jnp.where(first, part[2], part[3])]
            odd = [jnp.where(first, part[1], part[0]), jnp.where(first, part[3], part[2])]
            send[p, 0, :, 128 * a : 128 * a + 128] = jnp.concatenate(even, axis=0).astype(BF16)
            send[p, 1, :, 128 * a : 128 * a + 128] = jnp.concatenate(odd, axis=0).astype(BF16)

    def start_one(p):
        for c in range(2):
            if p == SELF:
                pl.when(c != core)(block_copy(p, c).start)
            else:
                block_copy(p, c).start()

    def at_edge(p):
        target = (z + distance(p) + n_z) % n_z
        return jnp.logical_or(target == 0, target == n_z - 1)

    for s in range(n_s):
        filtered(0, s)
    for p in range(EARLY):
        pl.when(jnp.logical_not(at_edge(p)))(functools.partial(pack_one, p))

    pl.semaphore_wait(barrier, 4 + n_cut - 1 + not_first.astype(jnp.int32) + not_last.astype(jnp.int32))

    def halo_copy(side, peer):
        return pltpu.make_async_remote_copy(
            hsend.at[side], hrecv.at[side], halo_ssem.at[side], halo_rsem.at[side],
            device_id={"tile": peer}, device_id_type=MESH,
        )

    pl.when(not_first)(lambda: halo_copy(0, tile - 1).start())
    pl.when(not_last)(lambda: halo_copy(1, tile + 1).start())

    for p in range(EARLY):
        pl.when(jnp.logical_not(at_edge(p)))(functools.partial(start_one, p))

    @pl.when(not_first)
    def _():
        halo_copy(0, tile - 1).wait_send()
        halo_copy(1, tile - 1).wait_recv()

    @pl.when(not_last)
    def _():
        halo_copy(1, tile + 1).wait_send()
        halo_copy(0, tile + 1).wait_recv()

    fill_halo(level)
    for s in range(n_s):
        filtered(0, s)
    for p in range(EARLY):

        @pl.when(at_edge(p))
        def _():
            pack_one(p)
            start_one(p)

    stat_copies = []
    for i in range(1, n_tile):
        stat_copies.append(
            pltpu.make_async_remote_copy(
                stat, stats.at[i], stat_ssem.at[i], stat_rsem.at[i],
                device_id={"tile": (tile + i) % n_tile}, device_id_type=MESH,
            )
        )

    signal_tile(row_in, right)
    pl.semaphore_wait(row_in, 1)
    signal_tile(col_in.at[0], front)
    signal_tile(col_in.at[1], back)
    pl.semaphore_wait(col_in.at[0], 1)
    pl.semaphore_wait(col_in.at[1], 1)
    signal_tile(col_in.at[2], front)
    pl.semaphore_wait(col_in.at[2], 1)
    for copy in stat_copies:
        copy.start()

    for copy in stat_copies:
        copy.wait()
    total = stat[...]
    for i in range(1, n_tile):
        total = total + stats[i]
    bgs[...] = mean(total)
    delta[...] = bgs[...] - local[...]
    off = delta[0:4, :]
    parts = []
    for k in range(2):
        r, c = 8 * k, 16 + 8 * k
        part = raw[c : c + 4, :] + pltpu.roll(raw[r : r + 4, :] * off, 32, 1)
        part = part + pltpu.roll(raw[c + 4 : c + 8, :], 64, 1) + pltpu.roll(raw[r + 4 : r + 8, :] * off, 96, 1)
        parts.append(part)
    msg[...] = jnp.concatenate(parts, axis=0).astype(BF16)

    def msg_copy(p, c):
        target = 2 * ((z + distance(p) + n_z) % n_z) + c
        return pltpu.make_async_remote_copy(
            msg, msgs.at[p, core], msg_ssem.at[p, c], msg_rsem.at[p, core],
            device_id={"cuts": target}, device_id_type=MESH,
        )

    for p in range(EARLY):
        for c in range(2):
            msg_copy(p, c).start()

    level = fill_field(bgs)
    fill_halo(level)
    for q in range(1, n_z // 4):
        for s in range(n_s):
            filtered(q, s)
        for p in range(4 * q, 4 * q + 4):
            pack_one(p)
        for p in range(4 * q, 4 * q + 4):
            start_one(p)

    own = pltpu.make_async_copy(send.at[15, core], recv.at[15, core], osem)
    own.start()

    for load in small[2:]:
        load.wait()

    both = jnp.concatenate([amp[...].astype(F32).T, like[...].astype(F32).T], axis=0).astype(BF16)
    at = lax.broadcasted_iota(jnp.int32, (8, 512), 1)

    def tall(x):
        return jnp.concatenate([x] * 16, axis=0)

    def source_slice(pos, source_core, inner):
        dist = jnp.zeros_like(pos)
        for p in range(n_z):
            dist = jnp.where(pos == p, ORDER[p], dist)
        return 8 * ((z - dist + 2 * n_z) & (n_z - 1)) + 4 * source_core + inner

    inner = (at >> 2) & 3
    inner = inner + core * (1 - 2 * (inner & 1))
    slices = tall(source_slice(at >> 5, (at >> 4) & 1, inner))
    row_of = tall(at & 3)
    down_at = lax.broadcasted_iota(jnp.int32, (128, 512), 0)
    for r in range(4):
        pick = jnp.where(jnp.logical_and(slices == down_at, row_of == r), 1.0, 0.0).astype(BF16)
        wmat[256 * r : 256 * r + 256, :] = jnp.dot(both, pick, preferred_element_type=F32).astype(BF16)

    for i in range(2):
        absent = hrecv[i, 0].astype(F32) > 0.5 * ABSENT
        seen[n_row + 8 if i == 0 else 0 : n_row + 16 if i == 0 else 8, :] = (
            jnp.where(absent, 0.0, 1.0)
        )
    seen[8 : n_row + 8, :] = valid[...].astype(F32)
    seen[n_row + 16 : n_row + 24, :] = jnp.zeros((8, n_col), F32)
    window = seen[pl.ds(pl.multiple_of(8 * z, 8), 32), :]
    window = jnp.where(core == 0, window[0:24], pltpu.roll(window, 28, 0)[0:24])
    window = jnp.concatenate([window, jnp.zeros((24, 128), F32)], axis=1)
    for j in range(TAPS):
        turned = pltpu.roll(window, (REACH - j) % (n_col + 128), 1) if j != REACH else window
        shifted[24 * j : 24 * j + 24, :] = turned[:, 0:n_col]
    shifted[24 * TAPS : 512, :] = jnp.zeros((512 - 24 * TAPS, n_col), F32)

    for p in range(EARLY):
        for c in range(2):
            msg_copy(p, c).wait_send()
            pltpu.make_async_remote_copy(
                msg, msgs.at[p, c], msg_ssem.at[p, c], msg_rsem.at[p, c],
                device_id={"cuts": me}, device_id_type=MESH,
            ).wait_recv()

    column = jnp.zeros_like(at)
    for j in range(1, 22):
        column = column + jnp.where(at >= 24 * j, 1, 0)
    row = at - 24 * column
    column, row = tall(column), tall(row)
    terms = msgs[...].reshape(64, 128)

    def spread(lane_of):
        return jnp.dot(terms, jnp.where(down_at == lane_of, 1.0, 0.0).astype(BF16), preferred_element_type=F32)

    at = lax.broadcasted_iota(jnp.int32, (128, 64), 1)
    wanted = source_slice(at >> 4, (at >> 3) & 1, at & 3) == lax.broadcasted_iota(jnp.int32, (128, 64), 0)
    mixed = jnp.dot(both, jnp.where(wanted, 1.0, 0.0).astype(BF16), preferred_element_type=F32).astype(BF16)
    col_terms = [spread(column + 64 * k) for k in range(2)]
    for r in range(4):
        product = col_terms[0] * spread(32 + row - r) + col_terms[1] * spread(96 + row - r)
        gmat[256 * r : 256 * r + 256, :] = -jnp.dot(mixed, product.astype(BF16), preferred_element_type=F32)

    def finish(p):
        for c in range(2):

            def ended():
                block_copy(p, c).wait_send()
                pltpu.make_async_remote_copy(
                    send.at[p, c], recv.at[p, c], ssem.at[p, c], rsem.at[p, c],
                    device_id={"cuts": me}, device_id_type=MESH,
                ).wait_recv()

            if p == SELF:
                pl.when(c != core)(ended)
            else:
                ended()

    half = n_z // 2
    for p in range(half):
        finish(p)

    def correct(j, carry):
        lanes = pl.ds(pl.multiple_of(256 * j, 256), 256)
        early = jnp.dot(gmat[...].astype(BF16), shifted[:, lanes].astype(BF16), preferred_element_type=F32)
        part = recv[0:half, :, :, lanes].reshape(256, 256)
        acc[:, lanes] = early + jnp.dot(wmat[:, 0:256], part, preferred_element_type=F32)
        return carry

    lax.fori_loop(0, n_col // 256, correct, 0)

    own.wait()
    for p in range(half, n_z):
        finish(p)


def project_kernel(blocks, weights, acc, amp_out, like_out, amps, likes, sems):
    copies = []
    for j in range(4):
        part = blocks[8:16, :, :, 256 * j : 256 * j + 256].reshape(256, 256)
        both = jnp.dot(weights[:, 256:512], part, preferred_element_type=F32) + acc[:, 256 * j : 256 * j + 256]
        for r in range(4):
            amp_float = both[256 * r : 256 * r + 128]
            like_float = amp_float * both[256 * r + 128 : 256 * r + 256]
            at = pl.ds(1024 * r + 256 * j, 256)
            amps[:, at] = amp_float.astype(BF16)
            likes[:, at] = like_float.astype(BF16)
            for i, (kept, out) in enumerate(((amps, amp_out), (likes, like_out))):
                copy = pltpu.make_async_copy(kept.at[:, at], out.at[:, at], sems.at[i, j, r])
                copy.start()
                copies.append(copy)
    for copy in copies:
        copy.wait()


def per_device(density, valid, row_taps, col_taps, amp_matrix, like_matrix):
    vmem = pl.BlockSpec(memory_space=pltpu.VMEM)
    anywhere = pl.BlockSpec(memory_space=pl.ANY)
    dma = pltpu.SemaphoreType.DMA
    blocks, weights, acc = pl.pallas_call(
        exchange_kernel,
        out_shape=(
            pltpu.VMEM((16, 2, 16, 1024), BF16),
            pltpu.VMEM((1024, 512), BF16),
            pltpu.VMEM((1024, 1024), F32),
        ),
        in_specs=[pl.BlockSpec(memory_space=pltpu.HBM)] * 6,
        out_specs=(vmem, vmem, vmem),
        scratch_shapes=[
            pltpu.VMEM((4, 128, 1024), BF16),
            pltpu.VMEM((128, 1024), jnp.int32),
            pltpu.VMEM((4, 4, 17), BF16),
            pltpu.VMEM((4, 4, 17), BF16),
            pltpu.VMEM((128, 128), BF16),
            pltpu.VMEM((128, 128), BF16),
            pltpu.VMEM((32, 256), F32),
            pltpu.VMEM((4, 4, 128, 256), BF16),
            pltpu.VMEM((4, 128, 1024), BF16),
            pltpu.VMEM((4, 256, 1024), BF16),
            pltpu.VMEM((4, 8, 32, 1024), BF16),
            pltpu.VMEM((4, 8, 32, 128), F32),
            pltpu.VMEM((16, 2, 16, 1024), BF16),
            pltpu.VMEM((8, 128), F32),
            pltpu.VMEM((16, 8, 128), F32),
            pltpu.VMEM((8, 128), F32),
            pltpu.VMEM((2, 4, 8, 1024), BF16),
            pltpu.VMEM((2, 4, 8, 1024), BF16),
            pltpu.VMEM((32, 128), F32),
            pltpu.VMEM((8, 128), F32),
            pltpu.VMEM((8, 128), F32),
            pltpu.VMEM((8, 128), BF16),
            pltpu.VMEM((EARLY, 2, 8, 128), BF16),
            pltpu.VMEM((152, 1024), F32),
            pltpu.VMEM((512, 1024), F32),
            pltpu.VMEM((1024, 512), F32),
            dma((16,)), dma((16,)), dma((2,)), dma((2,)),
            dma((16, 2)), dma((16, 2)), dma, dma, dma((4,)), dma((4,)),
            pltpu.SemaphoreType.REGULAR, pltpu.SemaphoreType.REGULAR((3,)),
            dma((EARLY, 2)), dma((EARLY, 2)),
        ],
        compiler_params=pltpu.CompilerParams(
            collective_id=0, has_side_effects=True, vmem_limit_bytes=44 * 1024 * 1024
        ),
        name="filter_exchange",
    )(*(
        pltpu.with_memory_space_constraint(x, pltpu.HBM)
        for x in (density, valid, row_taps, col_taps, amp_matrix, like_matrix)
    ))
    out = jax.ShapeDtypeStruct((128, 4096), BF16)
    return pl.pallas_call(
        project_kernel,
        out_shape=(out, out),
        in_specs=[vmem] * 3,
        out_specs=(anywhere, anywhere),
        scratch_shapes=[pltpu.VMEM((128, 4096), BF16), pltpu.VMEM((128, 4096), BF16), dma((2, 4, 4))],
        compiler_params=pltpu.CompilerParams(vmem_limit_bytes=44 * 1024 * 1024),
        name="project",
    )(
        pltpu.with_memory_space_constraint(blocks, pltpu.VMEM),
        pltpu.with_memory_space_constraint(weights, pltpu.VMEM),
        pltpu.with_memory_space_constraint(acc, pltpu.VMEM),
    )


def solution(mesh):
    return jax.shard_map(
        per_device,
        mesh=mesh,
        in_specs=(
            P("cuts", "tile", None),
            P("tile", None),
            P(None, "cuts", None),
            P(None, "cuts", None),
            P(),
            P(),
        ),
        out_specs=(P(None, ("tile", "cuts")), P(None, ("tile", "cuts"))),
        check_vma=False,
    )
```

```python
import functools

import jax
import jax.numpy as jnp
from jax import lax
from jax.experimental import pallas as pl
from jax.experimental.pallas import tpu as pltpu
from jax.sharding import PartitionSpec as P

MESH = pl.DeviceIdType.MESH
REACH = 8
TAPS = 2 * REACH + 1
ABSENT = 1024.0
F32 = jnp.float32
BF16 = jnp.bfloat16

ORDER = (6, -6, 7, -7, 8, 5, -5, 4, -4, 3, -3, 2, -2, 1, -1, 0)
EARLY = 4
SELF = 15


def distance(p):
    return ORDER[p]


def exchange_kernel(
    dens_in, valid_in, rtap_in, ctap_in, amp_in, like_in,
    recv, wmat, acc,
    dens, valid, rtap, ctap, amp, like, base, rband, cband, field, wide, outs, send, stat, stats, bgs, hsend, hrecv,
    raw, local, delta, msg, msgs, seen, shifted, gmat,
    stat_ssem, stat_rsem, halo_ssem, halo_rsem, ssem, rsem, osem, vsem, dsem, small_sem, row_in, col_in, msg_ssem, msg_rsem,
):
    n_s, n_row, n_col = dens.shape
    n_tile, n_cut = lax.axis_size("tile"), lax.axis_size("cuts")
    n_z = n_cut // 2
    tile, me = lax.axis_index("tile"), lax.axis_index("cuts")
    z, core = me // 2, me % 2
    n_a = n_col // 128

    loads = [pltpu.make_async_copy(valid_in, valid, vsem)]
    loads += [pltpu.make_async_copy(dens_in.at[s], dens.at[s], dsem.at[s]) for s in range(n_s)]
    small = [(rtap_in, rtap), (ctap_in, ctap), (amp_in, amp), (like_in, like)]
    small = [pltpu.make_async_copy(a, b, small_sem.at[i]) for i, (a, b) in enumerate(small)]
    for load in small[:2] + loads + small[2:]:
        load.start()

    barrier = pltpu.get_barrier_semaphore()
    n_x = 4
    n_y = n_tile // n_x
    y, x = tile // n_x, tile % n_x
    left, right = n_x * y + (x + n_x - 1) % n_x, n_x * y + (x + 1) % n_x
    back, front = n_x * ((y + n_y - 1) % n_y) + x, n_x * ((y + 1) % n_y) + x
    def signal_tile(sem, peer):
        pl.semaphore_signal(sem, inc=1, device_id={"tile": peer}, device_id_type=MESH)

    for i in range(n_z // 2, -1, -1):
        for peer_z in (z + i, z + n_z - i)[: 1 if i % (n_z // 2) == 0 else 2]:
            for c in range(2 if i else 1):
                peer = 2 * (peer_z % n_z) + (c if i else 1 - core)
                pl.semaphore_signal(barrier, inc=1, device_id={"cuts": peer}, device_id_type=MESH)
    for peer in (left, right, back, front):
        signal_tile(barrier, peer)
    not_first, not_last = tile > 0, tile < n_tile - 1

    @pl.when(not_first)
    def _():
        signal_tile(barrier, tile - 1)

    @pl.when(not_last)
    def _():
        signal_tile(barrier, tile + 1)

    for load in small[:2]:
        load.wait()
    raw[...] = jnp.zeros_like(raw)
    for k in range(4):
        raw[4 * k : 4 * k + 4, 0:TAPS] = rtap[k].astype(F32)
        raw[16 + 4 * k : 20 + 4 * k, 0:TAPS] = ctap[k].astype(F32)
    base[...] = pltpu.roll(jnp.concatenate([raw[...], jnp.zeros_like(raw)], axis=1), 256 - REACH, 1)
    for s in range(n_s):
        field[s, n_row : 2 * n_row, :] = jnp.zeros((n_row, n_col), BF16)

    for load in loads:
        load.wait()

    def fold(x):
        x = x[0:8] + x[8:16]
        total = x[:, 0:128]
        for a in range(1, n_a):
            total = total + x[:, 128 * a : 128 * a + 128]
        return total

    def sum_rows(i, accs):
        rows = pl.ds(pl.multiple_of(i * 16, 16), 16)
        mask = valid[rows, :].astype(F32)
        out = [accs[s] + fold(dens[s, rows, :].astype(F32) * mask) for s in range(n_s)]
        return (*out, accs[n_s] + fold(mask))

    accs = lax.fori_loop(0, n_row // 16, sum_rows, tuple(jnp.zeros((8, 128), F32) for _ in range(n_s + 1)))
    stat[...] = jnp.zeros_like(stat)
    for s in range(n_s + 1):
        stat[s : s + 1, :] = jnp.sum(accs[s], axis=0, keepdims=True)

    def mean(total):
        total = jnp.broadcast_to(jnp.sum(total, axis=1, keepdims=True), (8, 128))
        return total / jnp.broadcast_to(total[n_s : n_s + 1, :], (8, 128))

    local[...] = mean(stat[...])

    top, low = valid[0:8, :] != 0, valid[n_row - 8 : n_row, :] != 0
    for s in range(n_s):
        hsend[0, s] = jnp.where(top, dens[s, 0:16, :].astype(F32)[0:8], ABSENT).astype(BF16)
        hsend[1, s] = jnp.where(low, dens[s, n_row - 16 : n_row, :].astype(F32)[8:16], ABSENT).astype(BF16)

    def build(k):
        for s in range(n_s):
            row = jnp.broadcast_to(base[pl.ds(4 * k + s, 1), :], (8, 256))
            row = pltpu.roll(row, 0, 1, stride=1, stride_axis=0)
            if s % 2:
                row = pltpu.roll(row, 4, 0)
            for p in range(0, n_z, 2):
                pair = [pltpu.roll(row, 8 * ((z + distance(p + i) + n_z) % n_z), 1) for i in range(2)]
                rows = pl.ds(pl.multiple_of(32 * k + 8 * (p % 4), 16), 16)
                rband[s, p // 4, rows, :] = jnp.concatenate(pair, axis=0).astype(BF16)
            col = jnp.broadcast_to(base[pl.ds(16 + 4 * k + s, 1), :], (8, 256))
            col = pltpu.roll(col, 0, 1, stride=1, stride_axis=0)
            lanes = pl.ds(pl.multiple_of(256 * k, 256), 256)
            for m in range(0, 16, 2):
                pair = [pltpu.roll(col, 8 * (m + i), 1) if m + i else col for i in range(2)]
                cband[s, 8 * m : 8 * m + 16, lanes] = jnp.concatenate(pair, axis=0).astype(BF16)

    for k in range(4):
        build(k)

    @pl.when(jnp.logical_not(not_last))
    def _():
        hrecv[0] = jnp.full((n_s, 8, n_col), ABSENT, BF16)

    @pl.when(jnp.logical_not(not_first))
    def _():
        hrecv[1] = jnp.full((n_s, 8, n_col), ABSENT, BF16)

    def fill_field(levels):
        def level(s):
            return jnp.concatenate([levels[pl.ds(s, 1), :]] * n_a, axis=1)

        def mask_rows(i, carry):
            rows = pl.ds(pl.multiple_of(i * 16, 16), 16)
            mask = valid[rows, :].astype(F32)
            for s in range(n_s):
                field[s, rows, :] = (mask * (dens[s, rows, :].astype(F32) - level(s))).astype(BF16)
            return carry

        lax.fori_loop(0, n_row // 16, mask_rows, 0)
        return level

    def fill_halo(level):
        for s in range(n_s):
            after, before = hrecv[0, s].astype(F32), hrecv[1, s].astype(F32)
            after = jnp.where(after > 0.5 * ABSENT, 0.0, after - level(s))
            before = jnp.where(before > 0.5 * ABSENT, 0.0, before - level(s))
            none = jnp.zeros((8, n_col), F32)
            field[s, n_row : n_row + 16, :] = jnp.concatenate([after, none], axis=0).astype(BF16)
            field[s, 2 * n_row - 16 : 2 * n_row, :] = jnp.concatenate([none, before], axis=0).astype(BF16)

    level = fill_field(local)

    def block_copy(p, c):
        target = 2 * ((z + distance(p) + n_z) % n_z) + c
        return pltpu.make_async_remote_copy(
            send.at[p, c], recv.at[p, core], ssem.at[p, c], rsem.at[p, core],
            device_id={"cuts": target}, device_id_type=MESH,
        )

    lane = lax.broadcasted_iota(jnp.int32, (32, 128), 1)
    first = lax.broadcasted_iota(jnp.int32, (8, 128), 0) < 4

    def filtered(q, s):
        rowed = jnp.dot(rband[s, q], field[s], preferred_element_type=F32)
        for k in range(4):
            tiles = [rowed[32 * k : 32 * k + 32, 128 * a : 128 * a + 128] for a in range(n_a)]
            for a in range(n_a):
                right = tiles[a + 1] if a + 1 < n_a else jnp.zeros((32, 128), F32)
                left = tiles[a - 1] if a else jnp.zeros((32, 128), F32)
                wide[s, a, :, 256 * k : 256 * k + 128] = tiles[a].astype(BF16)
                wide[s, a, :, 256 * k + 128 : 256 * k + 256] = jnp.where(lane < 64, right, left).astype(BF16)
        done = lax.dot_general(
            wide[s].reshape(32 * n_a, 1024), cband[s], (((1,), (1,)), ((), ())), preferred_element_type=F32
        )
        outs[s] = done.reshape(n_a, 32, 128)

    def pack_one(p):
        i = p % 4
        for a in range(n_a):
            part = [outs[s, a, 8 * i : 8 * i + 8, :] for s in range(n_s)]
            even = [jnp.where(first, part[0], part[1]), jnp.where(first, part[2], part[3])]
            odd = [jnp.where(first, part[1], part[0]), jnp.where(first, part[3], part[2])]
            send[p, 0, :, 128 * a : 128 * a + 128] = jnp.concatenate(even, axis=0).astype(BF16)
            send[p, 1, :, 128 * a : 128 * a + 128] = jnp.concatenate(odd, axis=0).astype(BF16)

    def start_one(p):
        for c in range(2):
            if p == SELF:
                pl.when(c != core)(block_copy(p, c).start)
            else:
                block_copy(p, c).start()

    def at_edge(p):
        target = (z + distance(p) + n_z) % n_z
        return jnp.logical_or(target == 0, target == n_z - 1)

    for s in range(n_s):
        filtered(0, s)
    for p in range(EARLY):
        pl.when(jnp.logical_not(at_edge(p)))(functools.partial(pack_one, p))

    pl.semaphore_wait(barrier, 4 + n_cut - 1 + not_first.astype(jnp.int32) + not_last.astype(jnp.int32))

    def halo_copy(side, peer):
        return pltpu.make_async_remote_copy(
            hsend.at[side], hrecv.at[side], halo_ssem.at[side], halo_rsem.at[side],
            device_id={"tile": peer}, device_id_type=MESH,
        )

    pl.when(not_first)(lambda: halo_copy(0, tile - 1).start())
    pl.when(not_last)(lambda: halo_copy(1, tile + 1).start())

    for p in range(EARLY):
        pl.when(jnp.logical_not(at_edge(p)))(functools.partial(start_one, p))

    @pl.when(not_first)
    def _():
        halo_copy(0, tile - 1).wait_send()
        halo_copy(1, tile - 1).wait_recv()

    @pl.when(not_last)
    def _():
        halo_copy(1, tile + 1).wait_send()
        halo_copy(0, tile + 1).wait_recv()

    fill_halo(level)
    for s in range(n_s):
        filtered(0, s)
    for p in range(EARLY):

        @pl.when(at_edge(p))
        def _():
            pack_one(p)
            start_one(p)

    stat_copies = []
    for i in range(1, n_tile):
        stat_copies.append(
            pltpu.make_async_remote_copy(
                stat, stats.at[i], stat_ssem.at[i], stat_rsem.at[i],
                device_id={"tile": (tile + i) % n_tile}, device_id_type=MESH,
            )
        )

    signal_tile(row_in, right)
    pl.semaphore_wait(row_in, 1)
    signal_tile(col_in.at[0], front)
    signal_tile(col_in.at[1], back)
    pl.semaphore_wait(col_in.at[0], 1)
    pl.semaphore_wait(col_in.at[1], 1)
    signal_tile(col_in.at[2], front)
    pl.semaphore_wait(col_in.at[2], 1)
    for copy in stat_copies:
        copy.start()

    for copy in stat_copies:
        copy.wait()
    total = stat[...]
    for i in range(1, n_tile):
        total = total + stats[i]
    bgs[...] = mean(total)
    delta[...] = bgs[...] - local[...]
    off = delta[0:4, :]
    parts = []
    for k in range(2):
        r, c = 8 * k, 16 + 8 * k
        part = raw[c : c + 4, :] + pltpu.roll(raw[r : r + 4, :] * off, 32, 1)
        part = part + pltpu.roll(raw[c + 4 : c + 8, :], 64, 1) + pltpu.roll(raw[r + 4 : r + 8, :] * off, 96, 1)
        parts.append(part)
    msg[...] = jnp.concatenate(parts, axis=0).astype(BF16)

    def msg_copy(p, c):
        target = 2 * ((z + distance(p) + n_z) % n_z) + c
        return pltpu.make_async_remote_copy(
            msg, msgs.at[p, core], msg_ssem.at[p, c], msg_rsem.at[p, core],
            device_id={"cuts": target}, device_id_type=MESH,
        )

    for p in range(EARLY):
        for c in range(2):
            msg_copy(p, c).start()

    level = fill_field(bgs)
    fill_halo(level)
    for q in range(1, n_z // 4):
        for s in range(n_s):
            filtered(q, s)
        for p in range(4 * q, 4 * q + 4):
            pack_one(p)
        for p in range(4 * q, 4 * q + 4):
            start_one(p)

    own = pltpu.make_async_copy(send.at[15, core], recv.at[15, core], osem)
    own.start()

    for load in small[2:]:
        load.wait()

    both = jnp.concatenate([amp[...].astype(F32).T, like[...].astype(F32).T], axis=0).astype(BF16)
    at = lax.broadcasted_iota(jnp.int32, (8, 512), 1)

    def tall(x):
        return jnp.concatenate([x] * 16, axis=0)

    def source_slice(pos, source_core, inner):
        dist = jnp.zeros_like(pos)
        for p in range(n_z):
            dist = jnp.where(pos == p, ORDER[p], dist)
        return 8 * ((z - dist + 2 * n_z) & (n_z - 1)) + 4 * source_core + inner

    inner = (at >> 2) & 3
    inner = inner + core * (1 - 2 * (inner & 1))
    slices = tall(source_slice(at >> 5, (at >> 4) & 1, inner))
    row_of = tall(at & 3)
    down_at = lax.broadcasted_iota(jnp.int32, (128, 512), 0)
    for r in range(4):
        pick = jnp.where(jnp.logical_and(slices == down_at, row_of == r), 1.0, 0.0).astype(BF16)
        wmat[256 * r : 256 * r + 256, :] = jnp.dot(both, pick, preferred_element_type=F32).astype(BF16)

    for i in range(2):
        absent = hrecv[i, 0].astype(F32) > 0.5 * ABSENT
        seen[n_row + 8 if i == 0 else 0 : n_row + 16 if i == 0 else 8, :] = (
            jnp.where(absent, 0.0, 1.0)
        )
    seen[8 : n_row + 8, :] = valid[...].astype(F32)
    seen[n_row + 16 : n_row + 24, :] = jnp.zeros((8, n_col), F32)
    window = seen[pl.ds(pl.multiple_of(8 * z, 8), 32), :]
    window = jnp.where(core == 0, window[0:24], pltpu.roll(window, 28, 0)[0:24])
    window = jnp.concatenate([window, jnp.zeros((24, 128), F32)], axis=1)
    for j in range(TAPS):
        turned = pltpu.roll(window, (REACH - j) % (n_col + 128), 1) if j != REACH else window
        shifted[24 * j : 24 * j + 24, :] = turned[:, 0:n_col]
    shifted[24 * TAPS : 512, :] = jnp.zeros((512 - 24 * TAPS, n_col), F32)

    for p in range(EARLY):
        for c in range(2):
            msg_copy(p, c).wait_send()
            pltpu.make_async_remote_copy(
                msg, msgs.at[p, c], msg_ssem.at[p, c], msg_rsem.at[p, c],
                device_id={"cuts": me}, device_id_type=MESH,
            ).wait_recv()

    column = jnp.zeros_like(at)
    for j in range(1, 22):
        column = column + jnp.where(at >= 24 * j, 1, 0)
    row = at - 24 * column
    column, row = tall(column), tall(row)
    terms = msgs[...].reshape(64, 128)

    def spread(lane_of):
        return jnp.dot(terms, jnp.where(down_at == lane_of, 1.0, 0.0).astype(BF16), preferred_element_type=F32)

    at = lax.broadcasted_iota(jnp.int32, (128, 64), 1)
    wanted = source_slice(at >> 4, (at >> 3) & 1, at & 3) == lax.broadcasted_iota(jnp.int32, (128, 64), 0)
    mixed = jnp.dot(both, jnp.where(wanted, 1.0, 0.0).astype(BF16), preferred_element_type=F32).astype(BF16)
    col_terms = [spread(column + 64 * k) for k in range(2)]
    for r in range(4):
        product = col_terms[0] * spread(32 + row - r) + col_terms[1] * spread(96 + row - r)
        gmat[256 * r : 256 * r + 256, :] = -jnp.dot(mixed, product.astype(BF16), preferred_element_type=F32)

    def finish(p):
        for c in range(2):

            def ended():
                block_copy(p, c).wait_send()
                pltpu.make_async_remote_copy(
                    send.at[p, c], recv.at[p, c], ssem.at[p, c], rsem.at[p, c],
                    device_id={"cuts": me}, device_id_type=MESH,
                ).wait_recv()

            if p == SELF:
                pl.when(c != core)(ended)
            else:
                ended()

    half = n_z // 2
    for p in range(half):
        finish(p)

    def correct(j, carry):
        lanes = pl.ds(pl.multiple_of(256 * j, 256), 256)
        early = jnp.dot(gmat[...].astype(BF16), shifted[:, lanes].astype(BF16), preferred_element_type=F32)
        part = recv[0:half, :, :, lanes].reshape(256, 256)
        acc[:, lanes] = early + jnp.dot(wmat[:, 0:256], part, preferred_element_type=F32)
        return carry

    lax.fori_loop(0, n_col // 256, correct, 0)

    own.wait()
    for p in range(half, n_z):
        finish(p)


def project_kernel(blocks, weights, acc, amp_out, like_out, amps, likes, sems):
    copies = []
    for j in range(4):
        part = blocks[8:16, :, :, 256 * j : 256 * j + 256].reshape(256, 256)
        both = jnp.dot(weights[:, 256:512], part, preferred_element_type=F32) + acc[:, 256 * j : 256 * j + 256]
        for r in range(4):
            amp_float = both[256 * r : 256 * r + 128]
            like_float = amp_float * both[256 * r + 128 : 256 * r + 256]
            at = pl.ds(1024 * r + 256 * j, 256)
            amps[:, at] = amp_float.astype(BF16)
            likes[:, at] = like_float.astype(BF16)
            for i, (kept, out) in enumerate(((amps, amp_out), (likes, like_out))):
                copy = pltpu.make_async_copy(kept.at[:, at], out.at[:, at], sems.at[i, j, r])
                copy.start()
                copies.append(copy)
    for copy in copies:
        copy.wait()


def per_device(density, valid, row_taps, col_taps, amp_matrix, like_matrix):
    vmem = pl.BlockSpec(memory_space=pltpu.VMEM)
    anywhere = pl.BlockSpec(memory_space=pl.ANY)
    dma = pltpu.SemaphoreType.DMA
    blocks, weights, acc = pl.pallas_call(
        exchange_kernel,
        out_shape=(
            pltpu.VMEM((16, 2, 16, 1024), BF16),
            pltpu.VMEM((1024, 512), BF16),
            pltpu.VMEM((1024, 1024), F32),
        ),
        in_specs=[pl.BlockSpec(memory_space=pltpu.HBM)] * 6,
        out_specs=(vmem, vmem, vmem),
        scratch_shapes=[
            pltpu.VMEM((4, 128, 1024), BF16),
            pltpu.VMEM((128, 1024), jnp.int32),
            pltpu.VMEM((4, 4, 17), BF16),
            pltpu.VMEM((4, 4, 17), BF16),
            pltpu.VMEM((128, 128), BF16),
            pltpu.VMEM((128, 128), BF16),
            pltpu.VMEM((32, 256), F32),
            pltpu.VMEM((4, 4, 128, 256), BF16),
            pltpu.VMEM((4, 128, 1024), BF16),
            pltpu.VMEM((4, 256, 1024), BF16),
            pltpu.VMEM((4, 8, 32, 1024), BF16),
            pltpu.VMEM((4, 8, 32, 128), F32),
            pltpu.VMEM((16, 2, 16, 1024), BF16),
            pltpu.VMEM((8, 128), F32),
            pltpu.VMEM((16, 8, 128), F32),
            pltpu.VMEM((8, 128), F32),
            pltpu.VMEM((2, 4, 8, 1024), BF16),
            pltpu.VMEM((2, 4, 8, 1024), BF16),
            pltpu.VMEM((32, 128), F32),
            pltpu.VMEM((8, 128), F32),
            pltpu.VMEM((8, 128), F32),
            pltpu.VMEM((8, 128), BF16),
            pltpu.VMEM((EARLY, 2, 8, 128), BF16),
            pltpu.VMEM((152, 1024), F32),
            pltpu.VMEM((512, 1024), F32),
            pltpu.VMEM((1024, 512), F32),
            dma((16,)), dma((16,)), dma((2,)), dma((2,)),
            dma((16, 2)), dma((16, 2)), dma, dma, dma((4,)), dma((4,)),
            pltpu.SemaphoreType.REGULAR, pltpu.SemaphoreType.REGULAR((3,)),
            dma((EARLY, 2)), dma((EARLY, 2)),
        ],
        compiler_params=pltpu.CompilerParams(
            collective_id=0, has_side_effects=True, vmem_limit_bytes=44 * 1024 * 1024
        ),
        name="filter_exchange",
    )(*(
        pltpu.with_memory_space_constraint(x, pltpu.HBM)
        for x in (density, valid, row_taps, col_taps, amp_matrix, like_matrix)
    ))
    out = jax.ShapeDtypeStruct((128, 4096), BF16)
    return pl.pallas_call(
        project_kernel,
        out_shape=(out, out),
        in_specs=[vmem] * 3,
        out_specs=(anywhere, anywhere),
        scratch_shapes=[pltpu.VMEM((128, 4096), BF16), pltpu.VMEM((128, 4096), BF16), dma((2, 4, 4))],
        compiler_params=pltpu.CompilerParams(vmem_limit_bytes=44 * 1024 * 1024),
        name="project",
    )(
        pltpu.with_memory_space_constraint(blocks, pltpu.VMEM),
        pltpu.with_memory_space_constraint(weights, pltpu.VMEM),
        pltpu.with_memory_space_constraint(acc, pltpu.VMEM),
    )


def solution(mesh):
    return jax.shard_map(
        per_device,
        mesh=mesh,
        in_specs=(
            P("cuts", "tile", None),
            P("tile", None),
            P(None, "cuts", None),
            P(None, "cuts", None),
            P(),
            P(),
        ),
        out_specs=(P(None, ("tile", "cuts")), P(None, ("tile", "cuts"))),
        check_vma=False,
    )
```
